32 devices in a mesh: span: 16 (over z, x, core), seq: 2 (over y).
Axes of the slice: x: 2, y: 2, z: 4, core: 2. Of those that a mesh axis runs over, the one named last changes fastest.
Arguments:
- tokens: bfloat16 [8192, 1024], P(('span', 'seq')), may hold values from -48 to 48
- w_qkv: bfloat16 [1024, 3072], P('span'), may hold values from -0.1875 to 0.1875
- w_out: bfloat16 [1024, 1024], replicated, may hold values from -0.1875 to 0.1875
- w_cross: bfloat16 [1024, 2048], replicated, may hold values from -0.1875 to 0.1875
- ln_gain: float32 [1024], replicated, may hold values from 0.5 to 1.5
- ln_bias: float32 [1024], replicated, may hold values from -3 to 3
- queries: bfloat16 [1024, 1024], replicated, may hold values from -144 to 144
Outputs:
- encoded: bfloat16 [8192, 1024], P(('span', 'seq'))
- cross_out: bfloat16 [1024, 1024], P('span')
The draws below stay inside these ranges and needn't reach their ends.
All inputs are finite; a program needn't handle non-finite values.
Results may differ from the reference program's by a relative error of at most 0.013.
The reference program's roundings to bfloat16 on the way count: a program that leaves them out, or rounds other values in their place, can miss the bound.
Values may be sent and summed in bfloat16 or wider, within the bound.
A program may use at most 128 MiB of HBM per device.

```python
import math
import jax
import jax.numpy as jnp
from jax import lax

D = 1024
H = 16
DH = 64
NQ = 1024
L = 512
SPANS = 16
TOKENS = 8192


def draw_tokens(key, part):
    values = jnp.clip(jax.random.normal(jax.random.fold_in(key, 11), (TOKENS, D), jnp.float32), -6.0, 6.0)
    return values.astype(jnp.bfloat16)


def draw_queries(key, part):
    query_scale = 43.6 / math.sqrt(DH)
    values = query_scale * jnp.clip(jax.random.normal(jax.random.fold_in(key, 23), (NQ, D), jnp.float32), -4.0, 4.0)
    return values.astype(jnp.bfloat16)


def block_scale(own_key, extent, shards, low, high):
    def one(position, parts):
        heights = jax.random.uniform(jax.random.fold_in(jax.random.fold_in(own_key, 6), position), (parts,), jnp.float32, low / len(shards), high / len(shards))
        return jnp.repeat(jnp.exp(heights), extent[position] // parts).reshape((-1,) + (1,) * (len(extent) - position - 1))

    factor_of = one(*shards[0])
    for cut in shards[1:]:
        factor_of = factor_of * one(*cut)
    return factor_of


def gaussian(own_key, extent, deviation, bound, pieces=(), dtype=jnp.bfloat16):
    result = jax.random.normal(own_key, extent, jnp.float32) * deviation
    if len(pieces) > 0:
        result = block_scale(own_key, extent, pieces, -0.22, 0.18) * result
    return jnp.clip(result, min=-bound, max=bound).astype(dtype)


def setup_inputs(seed: int = 0) -> dict:
    streams_of = jax.random.split(jax.random.key(seed), 8)
    tokens = draw_tokens(jax.random.fold_in(streams_of[7], 71), 0)
    w_qkv = gaussian(streams_of[1], (D, 3 * D), D ** -0.5, 0.1875, ((0, 16),))
    w_out = gaussian(streams_of[2], (D, D), D ** -0.5, 0.1875)
    w_cross = gaussian(streams_of[3], (D, 2 * D), D ** -0.5, 0.1875)
    ln_gain = jnp.clip(jax.random.uniform(streams_of[4], (D,), jnp.float32, 0.5, 1.5), 0.5, 1.5)
    ln_bias = gaussian(streams_of[5], (D,), 0.5, 3.0, (), jnp.float32)
    queries = draw_queries(jax.random.fold_in(streams_of[7], 71), 0)
    return dict(tokens=tokens, w_qkv=w_qkv, w_out=w_out, w_cross=w_cross, ln_gain=ln_gain, ln_bias=ln_bias, queries=queries)


score_scale = 0.125

def layer_norm(residual, ln_gain, ln_bias):
    center = residual - lax.optimization_barrier(jnp.mean(residual, -1, keepdims=True))
    spread = lax.optimization_barrier(jnp.mean(center * center, -1, keepdims=True))
    return center * lax.rsqrt(spread + 1e-05) * ln_gain + ln_bias

def head_attend(triple):
    scores = jnp.dot(triple[0], triple[1].T, preferred_element_type=jnp.float32) * score_scale
    peaks = lax.optimization_barrier(jnp.max(scores, -1, keepdims=True))
    powers = jnp.exp(scores - peaks)
    totals = lax.optimization_barrier(jnp.sum(powers, -1, keepdims=True))
    return (jnp.dot(powers.astype(jnp.bfloat16), triple[2], preferred_element_type=jnp.float32) / totals).astype(jnp.bfloat16)

def reference(tokens, w_qkv, w_out, w_cross, ln_gain, ln_bias, queries):

    def encode_span(span_tokens):
        projected = jnp.dot(span_tokens, w_qkv, preferred_element_type=jnp.float32).astype(jnp.bfloat16)
        per_head = jnp.transpose(projected.reshape(L, 3, H, DH), (2, 1, 0, 3))
        head_outputs = lax.map(lambda triple: head_attend((triple[0], triple[1], triple[2])), per_head)
        attn = jnp.transpose(head_outputs, (1, 0, 2)).reshape(L, D)
        residual = span_tokens.astype(jnp.float32) + jnp.dot(attn, w_out, preferred_element_type=jnp.float32)
        encoded = layer_norm(residual, ln_gain, ln_bias).astype(jnp.bfloat16)
        cross_kv = jnp.dot(encoded, w_cross, preferred_element_type=jnp.float32).astype(jnp.bfloat16)
        return (encoded, cross_kv)
    encoded, cross_kv = lax.map(encode_span, tokens.reshape(SPANS, L, D))
    cross_kv = cross_kv.reshape(TOKENS, 2 * D)
    key_heads = jnp.transpose(cross_kv[:, :D].reshape(TOKENS, H, DH), (1, 0, 2))
    value_heads = jnp.transpose(cross_kv[:, D:].reshape(TOKENS, H, DH), (1, 0, 2))
    query_heads = jnp.transpose(queries.reshape(NQ, H, DH), (1, 0, 2))
    cross_heads = lax.map(lambda triple: head_attend((triple[0], triple[1], triple[2])), (query_heads, key_heads, value_heads))
    cross_out = jnp.transpose(cross_heads, (1, 0, 2)).reshape(NQ, D)
    return (encoded.reshape(TOKENS, D), cross_out)
```

```python
import functools

import jax
import jax.numpy as jnp
from jax import lax
from jax.experimental import pallas as pl
from jax.experimental.pallas import tpu as pltpu
from jax.sharding import PartitionSpec as P

DH = 64
PAIR = 2 * DH
score_scale = 0.125
F32 = jnp.float32
BF16 = jnp.bfloat16
MESH = pl.DeviceIdType.MESH


def mm(a, b):
    return jnp.dot(a, b, preferred_element_type=F32)


def mm_t(a, b):
    return lax.dot_general(a, b, (((1,), (1,)), ((), ())), preferred_element_type=F32)


def pair_attend(query, key, value):
    lane = lax.broadcasted_iota(jnp.int32, (1, PAIR), 1)
    low = lane < DH
    low_f = jnp.where(low, 1.0, 0.0)
    low_b = low_f.astype(BF16)
    high_b = (1.0 - low_f).astype(BF16)
    scaled = query * jnp.asarray(score_scale, BF16)

    def one(own, other):
        scores = mm_t(scaled * own, key)
        peak = jnp.max(scores, -1, keepdims=True)
        probs = jnp.exp(scores - peak).astype(BF16)
        return mm(probs, value * own + other), peak

    first, first_peak = one(low_b, high_b)
    second, second_peak = one(high_b, low_b)
    numerator = jnp.where(low, first, second)
    total = pltpu.roll(jnp.where(low, second, first), DH, 1)
    return numerator, total, jnp.where(low, first_peak, second_peak)


def routes(Z):
    if Z == 4:
        return [
            [(0, [1]), (1, [], False), (2, [], True), (3, [], True)],
            [(1, [2, 0]), (0, [2, 3], False), (2, [0], False), (3, [], True)],
            [(2, [1, 3]), (3, [1, 0], False), (1, [3], False), (0, [], True)],
            [(3, [2]), (2, [], False), (1, [], True), (0, [], True)],
        ]
    return [
        [(z, [(z + k) % Z for k in range(1, Z)])] + [((z - k) % Z, [], False) for k in range(1, Z)]
        for z in range(Z)
    ]


def kernel(
    S, Q, NQ,
    tokens_ref, wqkv_ref, wout_ref, wcross_ref, gain_ref, bias_ref, queries_ref,
    enc_ref, out_ref,
    wbuf, tokall, qkv, wout, wc, qc, att, attn, res, kv_tx, kv, o_tx, l_tx, o_rx, l_rx,
    w_sem, local_sem, z_send, z_recv, x_send, x_recv, c_send, c_recv,
    tok_send, tok_recv, at_send, at_recv, kv_send, kv_recv, o_send, o_recv, l_send, l_recv,
):
    T, D = tokens_ref.shape
    R = wqkv_ref.shape[0]
    hcols = D // Q
    pairs = hcols // PAIR
    Z = S // 4
    G = D // PAIR
    own_rows = NQ // S
    n = S * Q
    plan = routes(Z)
    span = lax.axis_index("span")
    seq = lax.axis_index("seq")
    z = span // 4
    x = (span // 2) % 2
    c = span % 2
    member = span % G
    base = span - member
    flat = span * Q + seq

    w_loads = []
    for p in range(pairs):
        for j in range(3):
            copy = pltpu.make_async_copy(
                wqkv_ref.at[:, pl.ds(pl.multiple_of(j * D + seq * hcols + p * PAIR, PAIR), PAIR)],
                wbuf.at[p, z, x, c, :, pl.ds(j * PAIR, PAIR)],
                w_sem.at[p, j],
            )
            copy.start()
            w_loads.append(copy)

    loads = []

    def load(src, dst):
        copy = pltpu.make_async_copy(src, dst, local_sem.at[len(loads)])
        copy.start()
        loads.append(copy)
        return copy

    own_t = pl.ds(pl.multiple_of(seq * T, T), T)
    t_load = load(tokens_ref, tokall.at[own_t])

    barrier = pltpu.get_barrier_semaphore()

    def greet(to_span, to_seq):
        pl.semaphore_signal(
            barrier, inc=1, device_id={"span": to_span, "seq": to_seq}, device_id_type=MESH
        )

    x_peer = z * 4 + (1 - x) * 2 + c
    c_peer = z * 4 + x * 2 + (1 - c)

    for k in range(1, Z):
        greet((z + k) % Z * 4 + x * 2 + c, seq)
    greet(x_peer, seq)
    greet(c_peer, seq)
    for j in range(1, Q):
        greet(span, (seq + j) % Q)

    wo_load = load(wout_ref, wout)
    wc_loads = []
    for g in range(G):
        for half in range(2):
            wc_loads.append(
                load(
                    wcross_ref.at[:, pl.ds(half * D + g * PAIR, PAIR)],
                    wc.at[g, :, pl.ds(half * PAIR, PAIR)],
                )
            )
    q_load = load(queries_ref.at[:, pl.ds(pl.multiple_of(member * PAIR, PAIR), PAIR)], qc)
    pl.semaphore_wait(barrier, Z + Q)

    def remote(src, dst, ssem, rsem, to_span, to_seq):
        return pltpu.make_async_remote_copy(
            src_ref=src, dst_ref=dst, send_sem=ssem, recv_sem=rsem,
            device_id={"span": to_span, "seq": to_seq}, device_id_type=MESH,
        )

    def by_z(p, zz, to):
        unit = wbuf.at[p, zz, x, c]
        return remote(
            unit, unit, z_send.at[p, zz, to], z_recv.at[p, zz], to * 4 + x * 2 + c, seq
        )

    def by_x(p, zz, xx):
        unit = wbuf.at[p, zz, xx, c]
        return remote(unit, unit, x_send.at[p, zz], x_recv.at[p, zz], x_peer, seq)

    def by_c(p, xx, cc):
        units = wbuf.at[p, :, xx, cc]
        return remote(units, units, c_send.at[p, xx], c_recv.at[p, xx], c_peer, seq)

    def send_tokens(j):
        mine = tokall.at[own_t]
        return remote(mine, mine, tok_send.at[j], tok_recv.at[seq], span, (seq + j) % Q)

    def at_z(action):
        for zv in range(Z):
            @pl.when(z == zv)
            def _():
                action(zv, plan[zv])

    def own(p):
        if p >= pairs:
            return
        for copy in w_loads[3 * p:3 * p + 3]:
            copy.wait()

        def go(zv, steps):
            for to in steps[0][1]:
                by_z(p, zv, to).start()

        at_z(go)
        by_x(p, z, x).start()
        if p == 0:
            t_load.wait()
            for j in range(1, Q):
                send_tokens(j).start()

    def arrive(p, second):
        if p >= pairs:
            return

        def go(zv, steps):
            for zz, onward, late in steps[1:]:
                if late == second:
                    by_z(p, zz, zv).wait_recv()
                    for to in onward:
                        by_z(p, zz, to).start()
                    by_x(p, zz, x).start()

        at_z(go)
        if second:
            by_c(p, x, c).start()

    def cross_over(p):
        if p >= pairs:
            return
        for zz in range(Z):
            by_x(p, zz, 1 - x).wait_recv()
        by_c(p, 1 - x, c).start()

    def project(p, owner):
        trows = pl.ds(pl.multiple_of(owner * T, T), T)
        w = wbuf[p].reshape(D, 3 * PAIR)
        qkv[p, trows] = mm(tokall[trows], w).astype(BF16)

    def project_own(p):
        if p >= pairs:
            return
        for xx in range(2):
            by_c(p, xx, 1 - c).wait_recv()
        project(p, seq)

    def attend(p, rows):
        num, tot, _ = pair_attend(
            qkv[p, rows, :PAIR], qkv[p, :, PAIR:2 * PAIR], qkv[p, :, 2 * PAIR:]
        )
        att[rows, p * PAIR:(p + 1) * PAIR] = (num / tot).astype(BF16)

    def pair_copy(j, p, at, owner):
        cols = pl.ds(p * PAIR, PAIR)
        return remote(
            att.at[pl.ds(pl.multiple_of(owner * T, T), T), cols], attn.at[at, :, cols],
            at_send.at[j, p], at_recv.at[at, p], span, owner,
        )

    def project_rest(p):
        if p >= pairs:
            return
        for j in range(1, Q):
            project(p, (seq + j) % Q)

    def attend_all(p):
        if p >= pairs:
            return
        if p < pairs - 1:
            for i in range(Q // 2):
                attend(p, pl.ds(2 * i * T, 2 * T))
            for j in range(1, Q):
                pair_copy(j, p, seq, (seq + j) % Q).start()
        else:
            for j in range(1, Q):
                owner = (seq + j) % Q
                attend(p, pl.ds(pl.multiple_of(owner * T, T), T))
                pair_copy(j, p, seq, owner).start()
            attend(p, own_t)

    def tokens_arrive():
        for j in range(1, Q):
            other = (seq + j) % Q
            theirs = tokall.at[pl.ds(pl.multiple_of(other * T, T), T)]
            remote(theirs, theirs, tok_send.at[j], tok_recv.at[other], span, other).wait_recv()

    own(0)
    own(1)
    arrive(0, False)
    own(2)
    arrive(0, True)
    arrive(1, False)
    own(3)
    cross_over(0)
    arrive(1, True)
    project_own(0)
    arrive(2, False)
    cross_over(1)
    arrive(2, True)
    project_own(1)
    arrive(3, False)
    cross_over(2)
    tokens_arrive()
    project_rest(0)
    arrive(3, True)
    attend_all(0)
    project_own(2)
    project_rest(1)
    attend_all(1)
    cross_over(3)
    project_rest(2)
    attend_all(2)
    project_own(3)
    project_rest(3)
    attend_all(3)
    wo_load.wait()
    NT = 256

    def out_part(j_seq, first):
        wrows = pl.ds(pl.multiple_of(j_seq * hcols, hcols), hcols)

        def tile(i, carry):
            cols = pl.ds(pl.multiple_of(i * NT, NT), NT)
            if first:
                res[:, cols] = tokall[own_t, cols].astype(F32) + mm(att[own_t], wout[wrows, cols])
            else:
                res[:, cols] += mm(attn[j_seq], wout[wrows, cols])
            return carry

        lax.fori_loop(0, D // NT, tile, 0)

    out_part(seq, True)
    for j in range(1, Q):
        owner = (seq + j) % Q
        for p in range(hcols // PAIR):
            pair_copy(j, p, owner, owner).wait_recv()
        out_part(owner, False)
    LT = 64

    def norm(i, carry):
        rows = pl.ds(pl.multiple_of(i * LT, LT), LT)
        r = res[rows]
        center = r - jnp.mean(r, -1, keepdims=True)
        spread = jnp.mean(center * center, -1, keepdims=True)
        enc_ref[rows] = (
            center * lax.rsqrt(spread + 1e-05) * gain_ref[...] + bias_ref[...]
        ).astype(BF16)
        return carry

    lax.fori_loop(0, T // LT, norm, 0)

    for copy in wc_loads:
        copy.wait()

    def kv_copy(g, at):
        return remote(
            kv_tx.at[g], kv.at[pl.ds(pl.multiple_of(at * T, T), T)],
            kv_send.at[g], kv_recv.at[at], base + g, seq,
        )

    def kv_step(i, carry):
        g = (member + i) % G
        kv_tx[g] = mm(enc_ref[...], wc[g]).astype(BF16)
        kv_copy(g, member).start()
        return carry

    lax.fori_loop(1, G, kv_step, 0)
    kv[pl.ds(pl.multiple_of(member * T, T), T)] = mm(enc_ref[...], wc[member]).astype(BF16)
    q_load.wait()

    def kv_wait(i, carry):
        g = (member + i) % G
        kv_copy(g, g).wait_recv()
        return carry

    lax.fori_loop(1, G, kv_wait, 0)

    BQ = max(own_rows, min(128, NQ))
    nb = BQ // own_rows
    lane = lax.broadcasted_iota(jnp.int32, (own_rows, PAIR), 1)
    row = lax.broadcasted_iota(jnp.int32, (own_rows, PAIR), 0)
    diagonal = (lane % DH) == row

    def part_copies(r, s):
        to = r * Q + s
        return (
            remote(o_tx.at[r], o_rx.at[flat], o_send.at[to], o_recv.at[flat], r, s),
            remote(l_tx.at[r], l_rx.at[flat], l_send.at[to], l_recv.at[flat], r, s),
        )

    def cross(step, carry):
        i = ((z + 1) * (NQ // BQ) // Z + step) % (NQ // BQ)
        rows = pl.ds(pl.multiple_of(i * BQ, BQ), BQ)
        num, tot, peak = pair_attend(qc[rows], kv[:, :PAIR], kv[:, PAIR:])
        part = (num / tot).astype(BF16)
        lse = peak + jnp.log(tot)
        for b in range(nb):
            r = i * nb + b
            stat = jnp.sum(
                jnp.where(diagonal, lse[b * own_rows:(b + 1) * own_rows], 0.0), 0, keepdims=True
            )
            stat = jnp.broadcast_to(stat, (8, PAIR))
            o_tx[r] = part[b * own_rows:(b + 1) * own_rows]
            l_tx[r] = stat

            @pl.when(r == span)
            def _():
                o_rx[flat] = part[b * own_rows:(b + 1) * own_rows]
                l_rx[flat] = stat

            for s in range(Q):
                @pl.when(r * Q + s != flat)
                def _():
                    for copy in part_copies(r, s):
                        copy.start()
        return carry

    lax.fori_loop(0, NQ // BQ, cross, 0)

    def part_wait(i, carry):
        src = (flat + i) % n
        r = src // Q
        s = src % Q
        remote(o_tx.at[r], o_rx.at[src], o_send.at[src], o_recv.at[src], r, s).wait_recv()
        remote(l_tx.at[r], l_rx.at[src], l_send.at[src], l_recv.at[src], r, s).wait_recv()
        return carry

    lax.fori_loop(1, n, part_wait, 0)

    low = lane < DH

    def merge(g, carry):
        sources = [(a * G + g) * Q + s for a in range(S // G) for s in range(Q)]
        stats = [l_rx[src][0:1] for src in sources]
        top = functools.reduce(jnp.maximum, stats)
        weights = [jnp.exp(v - top) for v in stats]
        whole = functools.reduce(jnp.add, weights)
        total = jnp.zeros((own_rows, PAIR), F32)
        for src, weight in zip(sources, weights):
            spread = jnp.where(diagonal, weight / whole, 0.0)
            left = jnp.sum(jnp.where(low, spread, 0.0), 1, keepdims=True)
            right = jnp.sum(jnp.where(low, 0.0, spread), 1, keepdims=True)
            total += o_rx[src].astype(F32) * jnp.where(low, left, right)
        out_ref[:, pl.ds(pl.multiple_of(g * PAIR, PAIR), PAIR)] = total.astype(BF16)
        return carry

    lax.fori_loop(0, G, merge, 0)

    for j in range(1, Q):
        send_tokens(j).wait_send()
        for p in range(pairs):
            pair_copy(j, p, seq, (seq + j) % Q).wait_send()
    for p in range(pairs):
        def gone(zv, steps):
            for step in steps:
                for to in step[1]:
                    by_z(p, step[0], to).wait_send()

        at_z(gone)
        for zz in range(Z):
            by_x(p, zz, x).wait_send()
        for xx in range(2):
            by_c(p, xx, c).wait_send()

    def kv_sent(i, carry):
        kv_copy((member + i) % G, member).wait_send()
        return carry

    lax.fori_loop(1, G, kv_sent, 0)

    def part_sent(i, carry):
        to = (flat + i) % n
        for copy in part_copies(to // Q, to % Q):
            copy.wait_send()
        return carry

    lax.fori_loop(1, n, part_sent, 0)


def hand_over(enc_ref, part_ref, enc_out, part_out):
    enc_out[...] = enc_ref[...]
    part_out[...] = part_ref[...]


def solution(mesh):
    S = mesh.shape["span"]
    Q = mesh.shape["seq"]

    def per_device(tokens, w_qkv, w_out, w_cross, ln_gain, ln_bias, queries):
        T, D = tokens.shape
        NQ = queries.shape[0]
        R = w_qkv.shape[0]
        hcols = D // Q
        pairs = hcols // PAIR
        Z = S // 4
        G = D // PAIR
        own_rows = NQ // S
        any_spec = pl.BlockSpec(memory_space=pl.ANY)
        vmem_spec = pl.BlockSpec(memory_space=pltpu.VMEM)
        dma = pltpu.SemaphoreType.DMA
        n = S * Q
        results = pl.pallas_call(
            functools.partial(kernel, S, Q, NQ),
            out_shape=(
                jax.ShapeDtypeStruct((T, D), BF16),
                jax.ShapeDtypeStruct((own_rows, D), BF16),
            ),
            in_specs=[any_spec] * 4 + [vmem_spec] * 2 + [any_spec],
            out_specs=(vmem_spec, vmem_spec),
            scratch_shapes=[
                pltpu.VMEM((pairs, Z, 2, 2, R, 3 * PAIR), BF16),
                pltpu.VMEM((Q * T, D), BF16),
                pltpu.VMEM((pairs, Q * T, 3 * PAIR), BF16),
                pltpu.VMEM((D, D), BF16),
                pltpu.VMEM((G, D, 2 * PAIR), BF16),
                pltpu.VMEM((NQ, PAIR), BF16),
                pltpu.VMEM((Q * T, hcols), BF16),
                pltpu.VMEM((Q, T, hcols), BF16),
                pltpu.VMEM((T, D), F32),
                pltpu.VMEM((G, T, 2 * PAIR), BF16),
                pltpu.VMEM((G * T, 2 * PAIR), BF16),
                pltpu.VMEM((S, own_rows, PAIR), BF16),
                pltpu.VMEM((S, 8, PAIR), F32),
                pltpu.VMEM((n, own_rows, PAIR), BF16),
                pltpu.VMEM((n, 8, PAIR), F32),
                dma((pairs, 3)), dma((3 + 2 * G,)),
                dma((pairs, Z, Z)), dma((pairs, Z)), dma((pairs, Z)), dma((pairs, Z)), dma((pairs, 2)), dma((pairs, 2)),
                dma((Q,)), dma((Q,)), dma((Q, pairs)), dma((Q, pairs)), dma((G,)), dma((G,)),
                dma((n,)), dma((n,)), dma((n,)), dma((n,)),
            ],
            compiler_params=pltpu.CompilerParams(
                collective_id=0, has_side_effects=True, vmem_limit_bytes=56 << 20
            ),
        )(tokens, w_qkv, w_out, w_cross, ln_gain.reshape(1, D), ln_bias.reshape(1, D), queries)
        return pl.pallas_call(
            hand_over,
            out_shape=tuple(jax.ShapeDtypeStruct(r.shape, r.dtype) for r in results),
            in_specs=[vmem_spec] * 2,
            out_specs=(vmem_spec, vmem_spec),
        )(*results)

    in_specs = (P(("span", "seq"), None), P("span", None), P(), P(), P(), P(), P())
    out_specs = (P(("span", "seq"), None), P("span", None))
    return jax.shard_map(
        per_device, mesh=mesh, in_specs=in_specs, out_specs=out_specs, check_vma=False
    )
```

```python
import functools

import jax
import jax.numpy as jnp
from jax import lax
from jax.experimental import pallas as pl
from jax.experimental.pallas import tpu as pltpu
from jax.sharding import PartitionSpec as P

DH = 64
PAIR = 2 * DH
score_scale = 0.125
F32 = jnp.float32
BF16 = jnp.bfloat16
MESH = pl.DeviceIdType.MESH
ORDER = (0, 1, 2, 4, 7, 3, 5, 6)
SPLIT = 5


def mm(a, b):
    return jnp.dot(a, b, preferred_element_type=F32)


def mm_t(a, b):
    return lax.dot_general(a, b, (((1,), (1,)), ((), ())), preferred_element_type=F32)


def pair_attend(query, key, value):
    lane = lax.broadcasted_iota(jnp.int32, (1, PAIR), 1)
    low = lane < DH
    low_f = jnp.where(low, 1.0, 0.0)
    low_b = low_f.astype(BF16)
    high_b = (1.0 - low_f).astype(BF16)
    scaled = query * jnp.asarray(score_scale, BF16)

    def one(own, other):
        scores = mm_t(scaled * own, key)
        peak = jnp.max(scores, -1, keepdims=True)
        probs = jnp.exp(scores - peak).astype(BF16)
        return mm(probs, value * own + other), peak

    first, first_peak = one(low_b, high_b)
    second, second_peak = one(high_b, low_b)
    numerator = jnp.where(low, first, second)
    total = pltpu.roll(jnp.where(low, second, first), DH, 1)
    return numerator, total, jnp.where(low, first_peak, second_peak)


def routes(Z):
    if Z == 4:
        return [
            [(0, [1]), (1, [], False), (2, [], True), (3, [], True)],
            [(1, [2, 0]), (0, [2, 3], False), (2, [0], False), (3, [], True)],
            [(2, [1, 3]), (3, [1, 0], False), (1, [3], False), (0, [], True)],
            [(3, [2]), (2, [], False), (1, [], True), (0, [], True)],
        ]
    return [
        [(z, [(z + k) % Z for k in range(1, Z)])] + [((z - k) % Z, [], False) for k in range(1, Z)]
        for z in range(Z)
    ]


def kernel(
    S, Q, NQ,
    tokens_ref, wqkv_ref, wout_ref, wcross_ref, gain_ref, bias_ref, queries_ref,
    enc_ref, out_ref,
    wbuf, tokall, qkv, wout, wc, qc, att, attn, res, kv_tx, kv,
    early_num, early_tot, early_peak, o_tx, l_tx, o_rx, l_rx,
    w_sem, local_sem, z_send, z_recv, x_send, x_recv, c_send, c_recv,
    tok_send, tok_recv, at_send, at_recv, kv_send, kv_recv, f_send, f_recv,
    o_send, o_recv, l_send, l_recv,
):
    T, D = tokens_ref.shape
    R = wqkv_ref.shape[0]
    hcols = D // Q
    pairs = hcols // PAIR
    Z = S // 4
    G = D // PAIR
    own_rows = NQ // S
    n = S * Q
    plan = routes(Z)
    span = lax.axis_index("span")
    seq = lax.axis_index("seq")
    z = span // 4
    x = (span // 2) % 2
    c = span % 2
    my_z = z % 2
    my_s = seq % 2
    member = my_z * 4 + x * 2 + my_s
    base = span - span % G
    flat = span * Q + seq

    w_loads = []
    for p in range(pairs):
        for j in range(3):
            copy = pltpu.make_async_copy(
                wqkv_ref.at[:, pl.ds(pl.multiple_of(j * D + seq * hcols + p * PAIR, PAIR), PAIR)],
                wbuf.at[p, z, x, c, :, pl.ds(j * PAIR, PAIR)],
                w_sem.at[p, j],
            )
            copy.start()
            w_loads.append(copy)

    loads = []

    def load(src, dst):
        copy = pltpu.make_async_copy(src, dst, local_sem.at[len(loads)])
        copy.start()
        loads.append(copy)
        return copy

    own_t = pl.ds(pl.multiple_of(seq * T, T), T)
    t_load = load(tokens_ref, tokall.at[own_t])

    barrier = pltpu.get_barrier_semaphore()

    def greet(to_span, to_seq):
        pl.semaphore_signal(
            barrier, inc=1, device_id={"span": to_span, "seq": to_seq}, device_id_type=MESH
        )

    x_peer = z * 4 + (1 - x) * 2 + c
    c_peer = z * 4 + x * 2 + (1 - c)

    for k in range(1, Z):
        greet((z + k) % Z * 4 + x * 2 + c, seq)
    greet(x_peer, seq)
    greet(c_peer, seq)
    for j in range(1, Q):
        greet(span, (seq + j) % Q)

    wo_load = load(wout_ref, wout)
    wc_loads = []
    for g in range(G):
        for half in range(2):
            wc_loads.append(
                load(
                    wcross_ref.at[:, pl.ds(half * D + g * PAIR, PAIR)],
                    wc.at[g, :, pl.ds(half * PAIR, PAIR)],
                )
            )
    q_load = load(
        queries_ref.at[
            pl.ds(pl.multiple_of(c * (NQ // 2), NQ // 2), NQ // 2),
            pl.ds(pl.multiple_of(member * PAIR, PAIR), PAIR),
        ],
        qc,
    )
    pl.semaphore_wait(barrier, Z + Q)

    def remote(src, dst, ssem, rsem, to_span, to_seq):
        return pltpu.make_async_remote_copy(
            src_ref=src, dst_ref=dst, send_sem=ssem, recv_sem=rsem,
            device_id={"span": to_span, "seq": to_seq}, device_id_type=MESH,
        )

    def by_z(p, zz, to):
        unit = wbuf.at[p, zz, x, c]
        return remote(
            unit, unit, z_send.at[p, zz, to], z_recv.at[p, zz], to * 4 + x * 2 + c, seq
        )

    def by_x(p, zz, xx):
        unit = wbuf.at[p, zz, xx, c]
        return remote(unit, unit, x_send.at[p, zz], x_recv.at[p, zz], x_peer, seq)

    def by_c(p, xx, cc):
        units = wbuf.at[p, :, xx, cc]
        return remote(units, units, c_send.at[p, xx], c_recv.at[p, xx], c_peer, seq)

    def send_tokens(j):
        mine = tokall.at[own_t]
        return remote(mine, mine, tok_send.at[j], tok_recv.at[seq], span, (seq + j) % Q)

    def at_z(action):
        for zv in range(Z):
            @pl.when(z == zv)
            def _():
                action(zv, plan[zv])

    def own(p):
        if p >= pairs:
            return
        for copy in w_loads[3 * p:3 * p + 3]:
            copy.wait()

        def go(zv, steps):
            for to in steps[0][1]:
                by_z(p, zv, to).start()

        at_z(go)
        by_x(p, z, x).start()
        if p == 0:
            t_load.wait()
            for j in range(1, Q):
                send_tokens(j).start()

    def arrive(p, second):
        if p >= pairs:
            return

        def go(zv, steps):
            for zz, onward, late in steps[1:]:
                if late == second:
                    by_z(p, zz, zv).wait_recv()
                    for to in onward:
                        by_z(p, zz, to).start()
                    by_x(p, zz, x).start()

        at_z(go)
        if second:
            by_c(p, x, c).start()

    def cross_over(p):
        if p >= pairs:
            return
        for zz in range(Z):
            by_x(p, zz, 1 - x).wait_recv()
        by_c(p, 1 - x, c).start()

    def project(p, owner):
        trows = pl.ds(pl.multiple_of(owner * T, T), T)
        w = wbuf[p].reshape(D, 3 * PAIR)
        qkv[p, trows] = mm(tokall[trows], w).astype(BF16)

    def project_own(p):
        if p >= pairs:
            return
        for xx in range(2):
            by_c(p, xx, 1 - c).wait_recv()
        project(p, seq)

    def attend(p, rows):
        num, tot, _ = pair_attend(
            qkv[p, rows, :PAIR], qkv[p, :, PAIR:2 * PAIR], qkv[p, :, 2 * PAIR:]
        )
        att[rows, p * PAIR:(p + 1) * PAIR] = (num / tot).astype(BF16)

    def pair_copy(j, p, at, owner):
        cols = pl.ds(p * PAIR, PAIR)
        return remote(
            att.at[pl.ds(pl.multiple_of(owner * T, T), T), cols], attn.at[at, :, cols],
            at_send.at[j, p], at_recv.at[at, p], span, owner,
        )

    def project_rest(p):
        if p >= pairs:
            return
        for j in range(1, Q):
            project(p, (seq + j) % Q)

    def attend_all(p):
        if p >= pairs:
            return
        if p < pairs - 1:
            for i in range(Q // 2):
                attend(p, pl.ds(2 * i * T, 2 * T))
            for j in range(1, Q):
                pair_copy(j, p, seq, (seq + j) % Q).start()
        else:
            for j in range(1, Q):
                owner = (seq + j) % Q
                attend(p, pl.ds(pl.multiple_of(owner * T, T), T))
                pair_copy(j, p, seq, owner).start()
            attend(p, own_t)

    def tokens_arrive():
        for j in range(1, Q):
            other = (seq + j) % Q
            theirs = tokall.at[pl.ds(pl.multiple_of(other * T, T), T)]
            remote(theirs, theirs, tok_send.at[j], tok_recv.at[other], span, other).wait_recv()

    own(0)
    own(1)
    arrive(0, False)
    own(2)
    arrive(0, True)
    arrive(1, False)
    own(3)
    arrive(1, True)
    arrive(2, False)
    cross_over(0)
    arrive(2, True)
    arrive(3, False)
    cross_over(1)
    arrive(3, True)
    project_own(0)
    cross_over(2)
    project_own(1)
    tokens_arrive()
    project_rest(0)
    attend_all(0)
    project_own(2)
    project_rest(1)
    attend_all(1)
    cross_over(3)
    project_rest(2)
    attend_all(2)
    project_own(3)
    project_rest(3)
    attend_all(3)
    wo_load.wait()
    NT = 256

    def out_part(j_seq, first):
        wrows = pl.ds(pl.multiple_of(j_seq * hcols, hcols), hcols)

        def tile(i, carry):
            cols = pl.ds(pl.multiple_of(i * NT, NT), NT)
            if first:
                res[:, cols] = tokall[own_t, cols].astype(F32) + mm(att[own_t], wout[wrows, cols])
            else:
                res[:, cols] += mm(attn[j_seq], wout[wrows, cols])
            return carry

        lax.fori_loop(0, D // NT, tile, 0)

    out_part(seq, True)
    for j in range(1, Q):
        owner = (seq + j) % Q
        for p in range(hcols // PAIR):
            pair_copy(j, p, owner, owner).wait_recv()
        out_part(owner, False)
    LT = 64

    def norm(i, carry):
        rows = pl.ds(pl.multiple_of(i * LT, LT), LT)
        r = res[rows]
        center = r - jnp.mean(r, -1, keepdims=True)
        spread = jnp.mean(center * center, -1, keepdims=True)
        enc_ref[rows] = (
            center * lax.rsqrt(spread + 1e-05) * gain_ref[...] + bias_ref[...]
        ).astype(BF16)
        return carry

    lax.fori_loop(0, T // LT, norm, 0)

    for copy in wc_loads:
        copy.wait()

    def chip_at(pos):
        flip = ORDER[pos]
        s1 = 1 - my_s if flip & 1 else my_s
        x1 = 1 - x if flip & 2 else x
        z1 = 1 - my_z if flip & 4 else my_z
        return z1 * 4 + x1 * 2 + s1, base + z1 * 4 + x1 * 2 + c, seq - my_s + s1

    def kv_copy(pos):
        _, to_span, to_seq = chip_at(pos)
        return remote(
            kv_tx.at[pos], kv.at[pos, c], kv_send.at[pos], kv_recv.at[pos], to_span, to_seq
        )

    def core_copy(pos, cc):
        block = kv.at[pos, cc]
        return remote(block, block, f_send.at[pos], f_recv.at[pos], c_peer, seq)

    for pos in range(1, G):
        kv_tx[pos] = mm(enc_ref[...], wc[chip_at(pos)[0]]).astype(BF16)
        kv_copy(pos).start()
    kv[0, c] = mm(enc_ref[...], wc[member]).astype(BF16)
    core_copy(0, c).start()
    q_load.wait()

    def collect(first, last):
        for pos in range(max(first, 1), last):
            kv_copy(pos).wait_recv()
            core_copy(pos, c).start()
        for pos in range(first, last):
            core_copy(pos, 1 - c).wait_recv()

    half = NQ // 2
    BQ = max(own_rows, min(256, half))
    nb = BQ // own_rows
    tiles = half // BQ
    lane = lax.broadcasted_iota(jnp.int32, (own_rows, PAIR), 1)
    row = lax.broadcasted_iota(jnp.int32, (own_rows, PAIR), 0)
    diagonal = (lane % DH) == row
    source = span // 2 * Q + seq

    def part_copies(b, s):
        to = b * Q + s
        r = c * (S // 2) + b
        return (
            remote(o_tx.at[b], o_rx.at[source], o_send.at[to], o_recv.at[source], r, s),
            remote(l_tx.at[b], l_rx.at[source], l_send.at[to], l_recv.at[source], r, s),
        )

    def attend_over(rows, first, last):
        block = kv[first:last].reshape((last - first) * 2 * T, 2 * PAIR)
        return pair_attend(qc[rows], block[:, :PAIR], block[:, PAIR:])

    def early(i, carry):
        rows = pl.ds(pl.multiple_of(i * BQ, BQ), BQ)
        num, tot, peak = attend_over(rows, 0, SPLIT)
        early_num[rows] = num
        early_tot[rows] = tot
        early_peak[rows] = peak
        return carry

    def final(step, carry):
        i = step
        rows = pl.ds(pl.multiple_of(i * BQ, BQ), BQ)
        num, tot, peak = attend_over(rows, SPLIT, G)
        before = early_peak[rows]
        top = jnp.maximum(peak, before)
        old = jnp.exp(before - top)
        new = jnp.exp(peak - top)
        num = num * new + early_num[rows] * old
        tot = tot * new + early_tot[rows] * old
        part = (num / tot).astype(BF16)
        lse = top + jnp.log(tot)
        for k in range(nb):
            b = i * nb + k
            r = c * (S // 2) + b
            stat = jnp.sum(
                jnp.where(diagonal, lse[k * own_rows:(k + 1) * own_rows], 0.0), 0, keepdims=True
            )
            o_tx[b] = part[k * own_rows:(k + 1) * own_rows]
            l_tx[b] = stat

            @pl.when(r == span)
            def _():
                o_rx[source] = part[k * own_rows:(k + 1) * own_rows]
                l_rx[source] = stat

            for s in range(Q):
                @pl.when(r * Q + s != flat)
                def _():
                    for copy in part_copies(b, s):
                        copy.start()
        return carry

    collect(0, SPLIT)
    lax.fori_loop(0, tiles, early, 0)
    collect(SPLIT, G)
    lax.fori_loop(0, tiles, final, 0)

    senders = n // 2

    def part_wait(src, carry):
        sender = src // Q * 2 + span // (S // 2)

        @pl.when(sender * Q + src % Q != flat)
        def _():
            remote(o_tx.at[0], o_rx.at[src], o_send.at[src], o_recv.at[src], c_peer, seq).wait_recv()
            remote(l_tx.at[0], l_rx.at[src], l_send.at[src], l_recv.at[src], c_peer, seq).wait_recv()

        return carry

    lax.fori_loop(0, senders, part_wait, 0)

    low = lane < DH

    def merge(g, carry):
        sources = [
            (a * (G // 2) + g // 2) * Q + s * 2 + g % 2 for a in range(S // G) for s in range(Q // 2)
        ]
        stats = [l_rx[src] for src in sources]
        top = functools.reduce(jnp.maximum, stats)
        weights = [jnp.exp(v - top) for v in stats]
        whole = functools.reduce(jnp.add, weights)
        total = jnp.zeros((own_rows, PAIR), F32)
        for src, weight in zip(sources, weights):
            spread = jnp.where(diagonal, weight / whole, 0.0)
            left = jnp.sum(jnp.where(low, spread, 0.0), 1, keepdims=True)
            right = jnp.sum(jnp.where(low, 0.0, spread), 1, keepdims=True)
            total += o_rx[src].astype(F32) * jnp.where(low, left, right)
        out_ref[:, pl.ds(pl.multiple_of(g * PAIR, PAIR), PAIR)] = total.astype(BF16)
        return carry

    lax.fori_loop(0, G, merge, 0)

    for j in range(1, Q):
        send_tokens(j).wait_send()
        for p in range(pairs):
            pair_copy(j, p, seq, (seq + j) % Q).wait_send()
    for p in range(pairs):
        def gone(zv, steps):
            for step in steps:
                for to in step[1]:
                    by_z(p, step[0], to).wait_send()

        at_z(gone)
        for zz in range(Z):
            by_x(p, zz, x).wait_send()
        for xx in range(2):
            by_c(p, xx, c).wait_send()
    for pos in range(G):
        if pos:
            kv_copy(pos).wait_send()
        core_copy(pos, c).wait_send()

    def part_sent(to, carry):
        b = to // Q
        s = to % Q

        @pl.when((c * (S // 2) + b) * Q + s != flat)
        def _():
            for copy in part_copies(b, s):
                copy.wait_send()

        return carry

    lax.fori_loop(0, senders, part_sent, 0)


def hand_over(enc_ref, part_ref, enc_out, part_out):
    enc_out[...] = enc_ref[...]
    part_out[...] = part_ref[...]


def solution(mesh):
    S = mesh.shape["span"]
    Q = mesh.shape["seq"]

    def per_device(tokens, w_qkv, w_out, w_cross, ln_gain, ln_bias, queries):
        T, D = tokens.shape
        NQ = queries.shape[0]
        R = w_qkv.shape[0]
        hcols = D // Q
        pairs = hcols // PAIR
        Z = S // 4
        G = D // PAIR
        own_rows = NQ // S
        any_spec = pl.BlockSpec(memory_space=pl.ANY)
        vmem_spec = pl.BlockSpec(memory_space=pltpu.VMEM)
        dma = pltpu.SemaphoreType.DMA
        n = S * Q
        results = pl.pallas_call(
            functools.partial(kernel, S, Q, NQ),
            out_shape=(
                jax.ShapeDtypeStruct((T, D), BF16),
                jax.ShapeDtypeStruct((own_rows, D), BF16),
            ),
            in_specs=[any_spec] * 4 + [vmem_spec] * 2 + [any_spec],
            out_specs=(vmem_spec, vmem_spec),
            scratch_shapes=[
                pltpu.VMEM((pairs, Z, 2, 2, R, 3 * PAIR), BF16),
                pltpu.VMEM((Q * T, D), BF16),
                pltpu.VMEM((pairs, Q * T, 3 * PAIR), BF16),
                pltpu.VMEM((D, D), BF16),
                pltpu.VMEM((G, D, 2 * PAIR), BF16),
                pltpu.VMEM((NQ // 2, PAIR), BF16),
                pltpu.VMEM((Q * T, hcols), BF16),
                pltpu.VMEM((Q, T, hcols), BF16),
                pltpu.VMEM((T, D), F32),
                pltpu.VMEM((G, T, 2 * PAIR), BF16),
                pltpu.VMEM((G, 2, T, 2 * PAIR), BF16),
                pltpu.VMEM((NQ // 2, PAIR), F32),
                pltpu.VMEM((NQ // 2, PAIR), F32),
                pltpu.VMEM((NQ // 2, PAIR), F32),
                pltpu.VMEM((S // 2, own_rows, PAIR), BF16),
                pltpu.VMEM((S // 2, 1, PAIR), F32),
                pltpu.VMEM((n // 2, own_rows, PAIR), BF16),
                pltpu.VMEM((n // 2, 1, PAIR), F32),
                dma((pairs, 3)), dma((3 + 2 * G,)),
                dma((pairs, Z, Z)), dma((pairs, Z)), dma((pairs, Z)), dma((pairs, Z)), dma((pairs, 2)), dma((pairs, 2)),
                dma((Q,)), dma((Q,)), dma((Q, pairs)), dma((Q, pairs)), dma((G,)), dma((G,)), dma((G,)), dma((G,)),
                dma((n // 2,)), dma((n // 2,)), dma((n // 2,)), dma((n // 2,)),
            ],
            compiler_params=pltpu.CompilerParams(
                collective_id=0, has_side_effects=True, vmem_limit_bytes=56 << 20
            ),
        )(tokens, w_qkv, w_out, w_cross, ln_gain.reshape(1, D), ln_bias.reshape(1, D), queries)
        return pl.pallas_call(
            hand_over,
            out_shape=tuple(jax.ShapeDtypeStruct(r.shape, r.dtype) for r in results),
            in_specs=[vmem_spec] * 2,
            out_specs=(vmem_spec, vmem_spec),
        )(*results)

    in_specs = (P(("span", "seq"), None), P("span", None), P(), P(), P(), P(), P())
    out_specs = (P(("span", "seq"), None), P("span", None))
    return jax.shard_map(
        per_device, mesh=mesh, in_specs=in_specs, out_specs=out_specs, check_vma=False
    )
```

```python
import functools

import jax
import jax.numpy as jnp
from jax import lax
from jax.experimental import pallas as pl
from jax.experimental.pallas import tpu as pltpu
from jax.sharding import PartitionSpec as P

DH = 64
PAIR = 2 * DH
score_scale = 0.125
F32 = jnp.float32
BF16 = jnp.bfloat16
MESH = pl.DeviceIdType.MESH
ORDER = (0, 4, 2, 1, 6, 7, 5, 3)
SPLIT = 5


def mm(a, b):
    return jnp.dot(a, b, preferred_element_type=F32)


def mm_t(a, b):
    return lax.dot_general(a, b, (((1,), (1,)), ((), ())), preferred_element_type=F32)


def pair_attend(query, key, value):
    lane = lax.broadcasted_iota(jnp.int32, (1, PAIR), 1)
    low = lane < DH
    low_f = jnp.where(low, 1.0, 0.0)
    low_b = low_f.astype(BF16)
    high_b = (1.0 - low_f).astype(BF16)
    scaled = query * jnp.asarray(score_scale, BF16)

    def one(own, other):
        scores = mm_t(scaled * own, key)
        peak = jnp.max(scores, -1, keepdims=True)
        probs = jnp.exp(scores - peak).astype(BF16)
        return mm(probs, value * own + other), peak

    first, first_peak = one(low_b, high_b)
    second, second_peak = one(high_b, low_b)
    numerator = jnp.where(low, first, second)
    total = pltpu.roll(jnp.where(low, second, first), DH, 1)
    return numerator, total, jnp.where(low, first_peak, second_peak)


def routes(Z):
    if Z == 4:
        return [
            [(0, [1]), (1, [], False), (2, [], True), (3, [], True)],
            [(1, [2, 0]), (0, [2, 3], False), (2, [0], False), (3, [], True)],
            [(2, [1, 3]), (3, [1, 0], False), (1, [3], False), (0, [], True)],
            [(3, [2]), (2, [], False), (1, [], True), (0, [], True)],
        ]
    return [
        [(z, [(z + k) % Z for k in range(1, Z)])] + [((z - k) % Z, [], False) for k in range(1, Z)]
        for z in range(Z)
    ]


def kernel(
    S, Q, NQ,
    tokens_ref, wqkv_ref, wout_ref, wcross_ref, gain_ref, bias_ref, queries_ref,
    enc_ref, out_ref,
    wbuf, tokall, qkv, wout, wc, qc, att, attn, res, kv_tx, kv,
    early_num, early_tot, early_peak, o_tx, l_tx, o_rx, l_rx,
    w_sem, local_sem, z_send, z_recv, x_send, x_recv, c_send, c_recv,
    tok_send, tok_recv, at_send, at_recv, kv_send, kv_recv, f_send, f_recv,
    o_send, o_recv, l_send, l_recv,
):
    T, D = tokens_ref.shape
    R = wqkv_ref.shape[0]
    hcols = D // Q
    pairs = hcols // PAIR
    Z = S // 4
    G = D // PAIR
    own_rows = NQ // S
    n = S * Q
    plan = routes(Z)
    span = lax.axis_index("span")
    seq = lax.axis_index("seq")
    z = span // 4
    x = (span // 2) % 2
    c = span % 2
    my_z = z % 2
    my_s = seq % 2
    member = my_z * 4 + x * 2 + my_s
    base = span - span % G
    flat = span * Q + seq

    w_loads = []
    for p in range(pairs):
        for j in range(3):
            copy = pltpu.make_async_copy(
                wqkv_ref.at[:, pl.ds(pl.multiple_of(j * D + seq * hcols + p * PAIR, PAIR), PAIR)],
                wbuf.at[p, z, x, c, :, pl.ds(j * PAIR, PAIR)],
                w_sem.at[p, j],
            )
            copy.start()
            w_loads.append(copy)

    loads = []

    def load(src, dst):
        copy = pltpu.make_async_copy(src, dst, local_sem.at[len(loads)])
        copy.start()
        loads.append(copy)
        return copy

    own_t = pl.ds(pl.multiple_of(seq * T, T), T)
    t_load = load(tokens_ref, tokall.at[own_t])

    barrier = pltpu.get_barrier_semaphore()

    def greet(to_span, to_seq):
        pl.semaphore_signal(
            barrier, inc=1, device_id={"span": to_span, "seq": to_seq}, device_id_type=MESH
        )

    x_peer = z * 4 + (1 - x) * 2 + c
    c_peer = z * 4 + x * 2 + (1 - c)

    for k in range(1, Z):
        greet((z + k) % Z * 4 + x * 2 + c, seq)
    greet(x_peer, seq)
    greet(c_peer, seq)
    for j in range(1, Q):
        greet(span, (seq + j) % Q)

    wo_load = load(wout_ref, wout)
    wc_loads = []
    for g in range(G):
        for half in range(2):
            wc_loads.append(
                load(
                    wcross_ref.at[:, pl.ds(half * D + g * PAIR, PAIR)],
                    wc.at[g, :, pl.ds(half * PAIR, PAIR)],
                )
            )
    q_load = load(
        queries_ref.at[
            pl.ds(pl.multiple_of(c * (NQ // 2), NQ // 2), NQ // 2),
            pl.ds(pl.multiple_of(member * PAIR, PAIR), PAIR),
        ],
        qc,
    )
    pl.semaphore_wait(barrier, Z + Q)

    def remote(src, dst, ssem, rsem, to_span, to_seq):
        return pltpu.make_async_remote_copy(
            src_ref=src, dst_ref=dst, send_sem=ssem, recv_sem=rsem,
            device_id={"span": to_span, "seq": to_seq}, device_id_type=MESH,
        )

    def by_z(p, zz, to):
        unit = wbuf.at[p, zz, x, c]
        return remote(
            unit, unit, z_send.at[p, zz, to], z_recv.at[p, zz], to * 4 + x * 2 + c, seq
        )

    def by_x(p, zz, xx):
        unit = wbuf.at[p, zz, xx, c]
        return remote(unit, unit, x_send.at[p, zz], x_recv.at[p, zz], x_peer, seq)

    def by_c(p, xx, cc):
        units = wbuf.at[p, :, xx, cc]
        return remote(units, units, c_send.at[p, xx], c_recv.at[p, xx], c_peer, seq)

    def send_tokens(j):
        mine = tokall.at[own_t]
        return remote(mine, mine, tok_send.at[j], tok_recv.at[seq], span, (seq + j) % Q)

    def at_z(action):
        for zv in range(Z):
            @pl.when(z == zv)
            def _():
                action(zv, plan[zv])

    def own(p):
        if p >= pairs:
            return
        for copy in w_loads[3 * p:3 * p + 3]:
            copy.wait()

        def go(zv, steps):
            for to in steps[0][1]:
                by_z(p, zv, to).start()

        at_z(go)
        by_x(p, z, x).start()
        if p == 0:
            t_load.wait()
            for j in range(1, Q):
                send_tokens(j).start()

    def arrive(p, second):
        if p >= pairs:
            return

        def go(zv, steps):
            for zz, onward, late in steps[1:]:
                if late == second:
                    by_z(p, zz, zv).wait_recv()
                    for to in onward:
                        by_z(p, zz, to).start()
                    by_x(p, zz, x).start()

        at_z(go)
        if second:
            by_c(p, x, c).start()

    def cross_over(p):
        if p >= pairs:
            return
        for zz in range(Z):
            by_x(p, zz, 1 - x).wait_recv()
        by_c(p, 1 - x, c).start()

    def project(p, owner):
        trows = pl.ds(pl.multiple_of(owner * T, T), T)
        w = wbuf[p].reshape(D, 3 * PAIR)
        qkv[p, trows] = mm(tokall[trows], w).astype(BF16)

    def project_own(p):
        if p >= pairs:
            return
        for xx in range(2):
            by_c(p, xx, 1 - c).wait_recv()
        if p < 2:
            project(p, seq)

    def attend(p, rows):
        num, tot, _ = pair_attend(
            qkv[p, rows, :PAIR], qkv[p, :, PAIR:2 * PAIR], qkv[p, :, 2 * PAIR:]
        )
        att[rows, p * PAIR:(p + 1) * PAIR] = (num / tot).astype(BF16)

    def pair_copy(j, p, at, owner):
        cols = pl.ds(p * PAIR, PAIR)
        return remote(
            att.at[pl.ds(pl.multiple_of(owner * T, T), T), cols], attn.at[at, :, cols],
            at_send.at[j, p], at_recv.at[at, p], span, owner,
        )

    def project_rest(p):
        if p >= pairs:
            return
        if p < 2:
            for j in range(1, Q):
                project(p, (seq + j) % Q)
        else:
            qkv[p] = mm(tokall[...], wbuf[p].reshape(D, 3 * PAIR)).astype(BF16)

    def attend_all(p):
        if p >= pairs:
            return
        if p < pairs - 1:
            for i in range(Q // 2):
                attend(p, pl.ds(2 * i * T, 2 * T))
            for j in range(1, Q):
                pair_copy(j, p, seq, (seq + j) % Q).start()
        else:
            for j in range(1, Q):
                owner = (seq + j) % Q
                attend(p, pl.ds(pl.multiple_of(owner * T, T), T))
                pair_copy(j, p, seq, owner).start()
            attend(p, own_t)

    def tokens_arrive():
        for j in range(1, Q):
            other = (seq + j) % Q
            theirs = tokall.at[pl.ds(pl.multiple_of(other * T, T), T)]
            remote(theirs, theirs, tok_send.at[j], tok_recv.at[other], span, other).wait_recv()

    own(0)
    own(1)
    arrive(0, False)
    own(2)
    arrive(0, True)
    arrive(1, False)
    own(3)
    arrive(1, True)
    arrive(2, False)
    cross_over(0)
    arrive(2, True)
    arrive(3, False)
    cross_over(1)
    arrive(3, True)
    project_own(0)
    cross_over(2)
    project_own(1)
    tokens_arrive()
    project_rest(0)
    attend_all(0)
    project_own(2)
    project_rest(1)
    attend_all(1)
    cross_over(3)
    project_rest(2)
    attend_all(2)
    project_own(3)
    project_rest(3)
    attend_all(3)
    wo_load.wait()
    NT = 256

    done = hcols - PAIR

    def wout_rows(j_seq, first, count):
        return pl.ds(pl.multiple_of(j_seq * hcols + first, PAIR), count)

    def own_part(i, carry):
        cols = pl.ds(pl.multiple_of(i * NT, NT), NT)
        part = mm(att[own_t], wout[wout_rows(seq, 0, hcols), cols])
        res[:, cols] = tokall[own_t, cols].astype(F32) + part
        return carry

    def their_part(owner, i, carry):
        cols = pl.ds(pl.multiple_of(i * NT, NT), NT)
        res[:, cols] += mm(attn[owner, :, :done], wout[wout_rows(owner, 0, done), cols])
        return carry

    lax.fori_loop(0, D // NT, own_part, 0)
    others = [(seq + j) % Q for j in range(1, Q)]
    for j, owner in enumerate(others, 1):
        for p in range(pairs - 1):
            pair_copy(j, p, owner, owner).wait_recv()
        if done:
            lax.fori_loop(0, D // NT, functools.partial(their_part, owner), 0)
    for j, owner in enumerate(others, 1):
        pair_copy(j, pairs - 1, owner, owner).wait_recv()
    LT = T // 2

    def norm(i, carry):
        rows = pl.ds(pl.multiple_of(i * LT, LT), LT)
        r = res[rows]
        for owner in others:
            r += mm(attn[owner, rows, done:], wout[wout_rows(owner, done, PAIR)])
        center = r - jnp.mean(r, -1, keepdims=True)
        spread = jnp.mean(center * center, -1, keepdims=True)
        enc_ref[rows] = (
            center * lax.rsqrt(spread + 1e-05) * gain_ref[...] + bias_ref[...]
        ).astype(BF16)
        return carry

    lax.fori_loop(0, T // LT, norm, 0)

    for copy in wc_loads:
        copy.wait()

    def chip_at(pos):
        flip = ORDER[pos]
        s1 = 1 - my_s if flip & 1 else my_s
        x1 = 1 - x if flip & 2 else x
        z1 = 1 - my_z if flip & 4 else my_z
        return z1 * 4 + x1 * 2 + s1, base + z1 * 4 + x1 * 2 + c, seq - my_s + s1

    def kv_copy(pos):
        _, to_span, to_seq = chip_at(pos)
        return remote(
            kv_tx.at[pos], kv.at[pos, c], kv_send.at[pos], kv_recv.at[pos], to_span, to_seq
        )

    def core_copy(pos, cc):
        block = kv.at[pos, cc]
        return remote(block, block, f_send.at[pos], f_recv.at[pos], c_peer, seq)

    for pos in range(1, G):
        kv_tx[pos] = mm(enc_ref[...], wc[chip_at(pos)[0]]).astype(BF16)
        kv_copy(pos).start()
    kv[0, c] = mm(enc_ref[...], wc[member]).astype(BF16)
    core_copy(0, c).start()
    q_load.wait()

    def collect(first, last):
        for pos in range(max(first, 1), last):
            kv_copy(pos).wait_recv()
            core_copy(pos, c).start()
        for pos in range(first, last):
            core_copy(pos, 1 - c).wait_recv()

    half = NQ // 2
    BQ = max(own_rows, min(256, half))
    nb = BQ // own_rows
    tiles = half // BQ
    lane = lax.broadcasted_iota(jnp.int32, (own_rows, PAIR), 1)
    row = lax.broadcasted_iota(jnp.int32, (own_rows, PAIR), 0)
    diagonal = (lane % DH) == row
    source = span // 2 * Q + seq

    def part_copies(b, s):
        to = b * Q + s
        r = c * (S // 2) + b
        return (
            remote(o_tx.at[b], o_rx.at[source], o_send.at[to], o_recv.at[source], r, s),
            remote(l_tx.at[b], l_rx.at[source], l_send.at[to], l_recv.at[source], r, s),
        )

    def attend_over(rows, first, last):
        block = kv[first:last].reshape((last - first) * 2 * T, 2 * PAIR)
        return pair_attend(qc[rows], block[:, :PAIR], block[:, PAIR:])

    def early(i, carry):
        rows = pl.ds(pl.multiple_of(i * BQ, BQ), BQ)
        num, tot, peak = attend_over(rows, 0, SPLIT)
        early_num[rows] = num
        early_tot[rows] = tot
        early_peak[rows] = peak
        return carry

    def final(step, carry):
        i = step
        rows = pl.ds(pl.multiple_of(i * BQ, BQ), BQ)
        num, tot, peak = attend_over(rows, SPLIT, G)
        before = early_peak[rows]
        top = jnp.maximum(peak, before)
        old = jnp.exp(before - top)
        new = jnp.exp(peak - top)
        num = num * new + early_num[rows] * old
        tot = tot * new + early_tot[rows] * old
        part = (num / tot).astype(BF16)
        lse = top + jnp.log(tot)
        for k in range(nb):
            b = i * nb + k
            r = c * (S // 2) + b
            stat = jnp.sum(
                jnp.where(diagonal, lse[k * own_rows:(k + 1) * own_rows], 0.0), 0, keepdims=True
            )
            o_tx[b] = part[k * own_rows:(k + 1) * own_rows]
            l_tx[b] = stat

            @pl.when(r == span)
            def _():
                o_rx[source] = part[k * own_rows:(k + 1) * own_rows]
                l_rx[source] = stat

            for s in range(Q):
                @pl.when(r * Q + s != flat)
                def _():
                    for copy in part_copies(b, s):
                        copy.start()
        return carry

    collect(0, SPLIT)
    lax.fori_loop(0, tiles, early, 0)
    collect(SPLIT, G)
    lax.fori_loop(0, tiles, final, 0)

    senders = n // 2

    def part_wait(src, carry):
        sender = src // Q * 2 + span // (S // 2)

        @pl.when(sender * Q + src % Q != flat)
        def _():
            remote(o_tx.at[0], o_rx.at[src], o_send.at[src], o_recv.at[src], c_peer, seq).wait_recv()
            remote(l_tx.at[0], l_rx.at[src], l_send.at[src], l_recv.at[src], c_peer, seq).wait_recv()

        return carry

    lax.fori_loop(0, senders, part_wait, 0)

    low = lane < DH

    def merge(g, carry):
        sources = [
            (a * (G // 2) + g // 2) * Q + s * 2 + g % 2 for a in range(S // G) for s in range(Q // 2)
        ]
        stats = [l_rx[src] for src in sources]
        top = functools.reduce(jnp.maximum, stats)
        weights = [jnp.exp(v - top) for v in stats]
        whole = functools.reduce(jnp.add, weights)
        total = jnp.zeros((own_rows, PAIR), F32)
        for src, weight in zip(sources, weights):
            spread = jnp.where(diagonal, weight / whole, 0.0)
            left = jnp.sum(jnp.where(low, spread, 0.0), 1, keepdims=True)
            right = jnp.sum(jnp.where(low, 0.0, spread), 1, keepdims=True)
            total += o_rx[src].astype(F32) * jnp.where(low, left, right)
        out_ref[:, pl.ds(pl.multiple_of(g * PAIR, PAIR), PAIR)] = total.astype(BF16)
        return carry

    lax.fori_loop(0, G, merge, 0)

    for j in range(1, Q):
        send_tokens(j).wait_send()
        for p in range(pairs):
            pair_copy(j, p, seq, (seq + j) % Q).wait_send()
    for p in range(pairs):
        def gone(zv, steps):
            for step in steps:
                for to in step[1]:
                    by_z(p, step[0], to).wait_send()

        at_z(gone)
        for zz in range(Z):
            by_x(p, zz, x).wait_send()
        for xx in range(2):
            by_c(p, xx, c).wait_send()
    for pos in range(G):
        if pos:
            kv_copy(pos).wait_send()
        core_copy(pos, c).wait_send()

    def part_sent(to, carry):
        b = to // Q
        s = to % Q

        @pl.when((c * (S // 2) + b) * Q + s != flat)
        def _():
            for copy in part_copies(b, s):
                copy.wait_send()

        return carry

    lax.fori_loop(0, senders, part_sent, 0)


def hand_over(enc_ref, part_ref, enc_out, part_out):
    enc_out[...] = enc_ref[...]
    part_out[...] = part_ref[...]


def solution(mesh):
    S = mesh.shape["span"]
    Q = mesh.shape["seq"]

    def per_device(tokens, w_qkv, w_out, w_cross, ln_gain, ln_bias, queries):
        T, D = tokens.shape
        NQ = queries.shape[0]
        R = w_qkv.shape[0]
        hcols = D // Q
        pairs = hcols // PAIR
        Z = S // 4
        G = D // PAIR
        own_rows = NQ // S
        any_spec = pl.BlockSpec(memory_space=pl.ANY)
        vmem_spec = pl.BlockSpec(memory_space=pltpu.VMEM)
        dma = pltpu.SemaphoreType.DMA
        n = S * Q
        results = pl.pallas_call(
            functools.partial(kernel, S, Q, NQ),
            out_shape=(
                jax.ShapeDtypeStruct((T, D), BF16),
                jax.ShapeDtypeStruct((own_rows, D), BF16),
            ),
            in_specs=[any_spec] * 4 + [vmem_spec] * 2 + [any_spec],
            out_specs=(vmem_spec, vmem_spec),
            scratch_shapes=[
                pltpu.VMEM((pairs, Z, 2, 2, R, 3 * PAIR), BF16),
                pltpu.VMEM((Q * T, D), BF16),
                pltpu.VMEM((pairs, Q * T, 3 * PAIR), BF16),
                pltpu.VMEM((D, D), BF16),
                pltpu.VMEM((G, D, 2 * PAIR), BF16),
                pltpu.VMEM((NQ // 2, PAIR), BF16),
                pltpu.VMEM((Q * T, hcols), BF16),
                pltpu.VMEM((Q, T, hcols), BF16),
                pltpu.VMEM((T, D), F32),
                pltpu.VMEM((G, T, 2 * PAIR), BF16),
                pltpu.VMEM((G, 2, T, 2 * PAIR), BF16),
                pltpu.VMEM((NQ // 2, PAIR), F32),
                pltpu.VMEM((NQ // 2, PAIR), F32),
                pltpu.VMEM((NQ // 2, PAIR), F32),
                pltpu.VMEM((S // 2, own_rows, PAIR), BF16),
                pltpu.VMEM((S // 2, 1, PAIR), F32),
                pltpu.VMEM((n // 2, own_rows, PAIR), BF16),
                pltpu.VMEM((n // 2, 1, PAIR), F32),
                dma((pairs, 3)), dma((3 + 2 * G,)),
                dma((pairs, Z, Z)), dma((pairs, Z)), dma((pairs, Z)), dma((pairs, Z)), dma((pairs, 2)), dma((pairs, 2)),
                dma((Q,)), dma((Q,)), dma((Q, pairs)), dma((Q, pairs)), dma((G,)), dma((G,)), dma((G,)), dma((G,)),
                dma((n // 2,)), dma((n // 2,)), dma((n // 2,)), dma((n // 2,)),
            ],
            compiler_params=pltpu.CompilerParams(
                collective_id=0, has_side_effects=True, vmem_limit_bytes=56 << 20
            ),
        )(tokens, w_qkv, w_out, w_cross, ln_gain.reshape(1, D), ln_bias.reshape(1, D), queries)
        return pl.pallas_call(
            hand_over,
            out_shape=tuple(jax.ShapeDtypeStruct(r.shape, r.dtype) for r in results),
            in_specs=[vmem_spec] * 2,
            out_specs=(vmem_spec, vmem_spec),
        )(*results)

    in_specs = (P(("span", "seq"), None), P("span", None), P(), P(), P(), P(), P())
    out_specs = (P(("span", "seq"), None), P("span", None))
    return jax.shard_map(
        per_device, mesh=mesh, in_specs=in_specs, out_specs=out_specs, check_vma=False
    )
```

```python
import functools

import jax
import jax.numpy as jnp
from jax import lax
from jax.experimental import pallas as pl
from jax.experimental.pallas import tpu as pltpu
from jax.sharding import PartitionSpec as P

DH = 64
PAIR = 2 * DH
score_scale = 0.125
F32 = jnp.float32
BF16 = jnp.bfloat16
MESH = pl.DeviceIdType.MESH
ORDER = (0, 4, 2, 1, 6, 7, 5, 3)
SPLIT = 4


def mm(a, b):
    return jnp.dot(a, b, preferred_element_type=F32)


def mm_t(a, b):
    return lax.dot_general(a, b, (((1,), (1,)), ((), ())), preferred_element_type=F32)


def pair_attend(query, key, value):
    lane = lax.broadcasted_iota(jnp.int32, (1, PAIR), 1)
    low = lane < DH
    low_f = jnp.where(low, 1.0, 0.0)
    low_b = low_f.astype(BF16)
    high_b = (1.0 - low_f).astype(BF16)
    scaled = query * jnp.asarray(score_scale, BF16)

    def one(own, other):
        scores = mm_t(scaled * own, key)
        peak = jnp.max(scores, -1, keepdims=True)
        probs = jnp.exp(scores - peak).astype(BF16)
        return mm(probs, value * own + other), peak

    first, first_peak = one(low_b, high_b)
    second, second_peak = one(high_b, low_b)
    numerator = jnp.where(low, first, second)
    total = pltpu.roll(jnp.where(low, second, first), DH, 1)
    return numerator, total, jnp.where(low, first_peak, second_peak)


def routes(Z):
    if Z == 4:
        return [
            [(0, [1]), (1, [], False), (2, [], True), (3, [], True)],
            [(1, [2, 0]), (0, [2, 3], False), (2, [0], False), (3, [], True)],
            [(2, [1, 3]), (3, [1, 0], False), (1, [3], False), (0, [], True)],
            [(3, [2]), (2, [], False), (1, [], True), (0, [], True)],
        ]
    return [
        [(z, [(z + k) % Z for k in range(1, Z)])] + [((z - k) % Z, [], False) for k in range(1, Z)]
        for z in range(Z)
    ]


def kernel(
    S, Q, NQ,
    tokens_ref, wqkv_ref, wout_ref, wcross_ref, gain_ref, bias_ref, queries_ref,
    enc_ref, out_ref,
    wbuf, tokall, qkv, wout, wc, qc, att, attn, res, kv_tx, kv,
    early_num, early_tot, early_peak, o_tx, l_tx, o_rx, l_rx,
    w_sem, local_sem, z_send, z_recv, x_send, x_recv, c_send, c_recv,
    tok_send, tok_recv, at_send, at_recv, kv_send, kv_recv, f_send, f_recv,
    o_send, o_recv, l_send, l_recv,
):
    T, D = tokens_ref.shape
    R = wqkv_ref.shape[0]
    hcols = D // Q
    pairs = hcols // PAIR
    Z = S // 4
    G = D // PAIR
    own_rows = NQ // S
    n = S * Q
    plan = routes(Z)
    span = lax.axis_index("span")
    seq = lax.axis_index("seq")
    z = span // 4
    x = (span // 2) % 2
    c = span % 2
    my_z = z % 2
    my_s = seq % 2
    member = my_z * 4 + x * 2 + my_s
    base = span - span % G
    flat = span * Q + seq

    w_loads = []
    for p in range(pairs):
        for j in range(3):
            copy = pltpu.make_async_copy(
                wqkv_ref.at[:, pl.ds(pl.multiple_of(j * D + seq * hcols + p * PAIR, PAIR), PAIR)],
                wbuf.at[p, z, x, c, :, pl.ds(j * PAIR, PAIR)],
                w_sem.at[p, j],
            )
            copy.start()
            w_loads.append(copy)

    loads = []

    def load(src, dst):
        copy = pltpu.make_async_copy(src, dst, local_sem.at[len(loads)])
        copy.start()
        loads.append(copy)
        return copy

    own_t = pl.ds(pl.multiple_of(seq * T, T), T)
    t_load = load(tokens_ref, tokall.at[own_t])

    barrier = pltpu.get_barrier_semaphore()

    def greet(to_span, to_seq):
        pl.semaphore_signal(
            barrier, inc=1, device_id={"span": to_span, "seq": to_seq}, device_id_type=MESH
        )

    x_peer = z * 4 + (1 - x) * 2 + c
    c_peer = z * 4 + x * 2 + (1 - c)

    for k in range(1, Z):
        greet((z + k) % Z * 4 + x * 2 + c, seq)
    greet(x_peer, seq)
    greet(c_peer, seq)
    for j in range(1, Q):
        greet(span, (seq + j) % Q)

    wo_load = load(wout_ref, wout)
    wc_loads = []
    for g in range(G):
        for half in range(2):
            wc_loads.append(
                load(
                    wcross_ref.at[:, pl.ds(half * D + g * PAIR, PAIR)],
                    wc.at[g, :, pl.ds(half * PAIR, PAIR)],
                )
            )
    q_load = load(
        queries_ref.at[
            pl.ds(pl.multiple_of(c * (NQ // 2), NQ // 2), NQ // 2),
            pl.ds(pl.multiple_of(member * PAIR, PAIR), PAIR),
        ],
        qc,
    )
    pl.semaphore_wait(barrier, Z + Q)

    def remote(src, dst, ssem, rsem, to_span, to_seq):
        return pltpu.make_async_remote_copy(
            src_ref=src, dst_ref=dst, send_sem=ssem, recv_sem=rsem,
            device_id={"span": to_span, "seq": to_seq}, device_id_type=MESH,
        )

    def by_z(p, zz, to):
        unit = wbuf.at[p, zz, x, c]
        return remote(
            unit, unit, z_send.at[p, zz, to], z_recv.at[p, zz], to * 4 + x * 2 + c, seq
        )

    def by_x(p, zz, xx):
        unit = wbuf.at[p, zz, xx, c]
        return remote(unit, unit, x_send.at[p, zz], x_recv.at[p, zz], x_peer, seq)

    def by_c(p, xx, cc):
        units = wbuf.at[p, :, xx, cc]
        return remote(units, units, c_send.at[p, xx], c_recv.at[p, xx], c_peer, seq)

    def send_tokens(j):
        mine = tokall.at[own_t]
        return remote(mine, mine, tok_send.at[j], tok_recv.at[seq], span, (seq + j) % Q)

    def at_z(action):
        for zv in range(Z):
            @pl.when(z == zv)
            def _():
                action(zv, plan[zv])

    def own(p):
        if p >= pairs:
            return
        for copy in w_loads[3 * p:3 * p + 3]:
            copy.wait()

        def go(zv, steps):
            for to in steps[0][1]:
                by_z(p, zv, to).start()

        at_z(go)
        by_x(p, z, x).start()
        if p == 0:
            t_load.wait()
            for j in range(1, Q):
                send_tokens(j).start()

    def arrive(p, second):
        if p >= pairs:
            return

        def go(zv, steps):
            for zz, onward, late in steps[1:]:
                if late == second:
                    by_z(p, zz, zv).wait_recv()
                    for to in onward:
                        by_z(p, zz, to).start()
                    by_x(p, zz, x).start()

        at_z(go)
        if second:
            by_c(p, x, c).start()

    def cross_over(p):
        if p >= pairs:
            return
        for zz in range(Z):
            by_x(p, zz, 1 - x).wait_recv()
        by_c(p, 1 - x, c).start()

    def project(p, owner):
        trows = pl.ds(pl.multiple_of(owner * T, T), T)
        w = wbuf[p].reshape(D, 3 * PAIR)
        qkv[p, trows] = mm(tokall[trows], w).astype(BF16)

    def project_own(p):
        if p >= pairs:
            return
        for xx in range(2):
            by_c(p, xx, 1 - c).wait_recv()
        if p < 2:
            project(p, seq)

    def attend(p, rows):
        num, tot, _ = pair_attend(
            qkv[p, rows, :PAIR], qkv[p, :, PAIR:2 * PAIR], qkv[p, :, 2 * PAIR:]
        )
        att[rows, p * PAIR:(p + 1) * PAIR] = (num / tot).astype(BF16)

    def pair_copy(j, p, at, owner):
        cols = pl.ds(p * PAIR, PAIR)
        return remote(
            att.at[pl.ds(pl.multiple_of(owner * T, T), T), cols], attn.at[at, :, cols],
            at_send.at[j, p], at_recv.at[at, p], span, owner,
        )

    def project_rest(p):
        if p >= pairs:
            return
        if p < 2:
            for j in range(1, Q):
                project(p, (seq + j) % Q)
        else:
            qkv[p] = mm(tokall[...], wbuf[p].reshape(D, 3 * PAIR)).astype(BF16)

    def attend_all(p):
        if p >= pairs:
            return
        if p < pairs - 1:
            for i in range(Q // 2):
                attend(p, pl.ds(2 * i * T, 2 * T))
            for j in range(1, Q):
                pair_copy(j, p, seq, (seq + j) % Q).start()
        else:
            for j in range(1, Q):
                owner = (seq + j) % Q
                attend(p, pl.ds(pl.multiple_of(owner * T, T), T))
                pair_copy(j, p, seq, owner).start()
            attend(p, own_t)

    def tokens_arrive():
        for j in range(1, Q):
            other = (seq + j) % Q
            theirs = tokall.at[pl.ds(pl.multiple_of(other * T, T), T)]
            remote(theirs, theirs, tok_send.at[j], tok_recv.at[other], span, other).wait_recv()

    own(0)
    own(1)
    arrive(0, False)
    own(2)
    arrive(0, True)
    arrive(1, False)
    own(3)
    arrive(1, True)
    arrive(2, False)
    cross_over(0)
    arrive(2, True)
    arrive(3, False)
    cross_over(1)
    arrive(3, True)
    project_own(0)
    cross_over(2)
    project_own(1)
    tokens_arrive()
    project_rest(0)
    attend_all(0)
    project_own(2)
    project_rest(1)
    attend_all(1)
    cross_over(3)
    project_rest(2)
    attend_all(2)
    project_own(3)
    project_rest(3)
    attend_all(3)
    wo_load.wait()
    NT = 256

    done = hcols - PAIR

    def wout_rows(j_seq, first, count):
        return pl.ds(pl.multiple_of(j_seq * hcols + first, PAIR), count)

    def own_part(i, carry):
        cols = pl.ds(pl.multiple_of(i * NT, NT), NT)
        part = mm(att[own_t], wout[wout_rows(seq, 0, hcols), cols])
        res[:, cols] = tokall[own_t, cols].astype(F32) + part
        return carry

    def their_part(owner, i, carry):
        cols = pl.ds(pl.multiple_of(i * NT, NT), NT)
        res[:, cols] += mm(attn[owner, :, :done], wout[wout_rows(owner, 0, done), cols])
        return carry

    lax.fori_loop(0, D // NT, own_part, 0, unroll=True)
    others = [(seq + j) % Q for j in range(1, Q)]
    for j, owner in enumerate(others, 1):
        for p in range(pairs - 1):
            pair_copy(j, p, owner, owner).wait_recv()
        if done:
            lax.fori_loop(0, D // NT, functools.partial(their_part, owner), 0, unroll=True)
    for j, owner in enumerate(others, 1):
        pair_copy(j, pairs - 1, owner, owner).wait_recv()
    LT = T // 2

    def norm(i, carry):
        rows = pl.ds(pl.multiple_of(i * LT, LT), LT)
        r = res[rows]
        for owner in others:
            r += mm(attn[owner, rows, done:], wout[wout_rows(owner, done, PAIR)])
        center = r - jnp.mean(r, -1, keepdims=True)
        spread = jnp.mean(center * center, -1, keepdims=True)
        enc_ref[rows] = (
            center * lax.rsqrt(spread + 1e-05) * gain_ref[...] + bias_ref[...]
        ).astype(BF16)
        return carry

    lax.fori_loop(0, T // LT, norm, 0, unroll=True)

    for copy in wc_loads:
        copy.wait()

    def chip_at(pos):
        flip = ORDER[pos]
        s1 = 1 - my_s if flip & 1 else my_s
        x1 = 1 - x if flip & 2 else x
        z1 = 1 - my_z if flip & 4 else my_z
        return z1 * 4 + x1 * 2 + s1, base + z1 * 4 + x1 * 2 + c, seq - my_s + s1

    def kv_copy(pos):
        _, to_span, to_seq = chip_at(pos)
        return remote(
            kv_tx.at[pos], kv.at[pos, c], kv_send.at[pos], kv_recv.at[pos], to_span, to_seq
        )

    def core_copy(pos, cc):
        block = kv.at[pos, cc]
        return remote(block, block, f_send.at[pos], f_recv.at[pos], c_peer, seq)

    for pos in range(1, G):
        kv_tx[pos] = mm(enc_ref[...], wc[chip_at(pos)[0]]).astype(BF16)
        kv_copy(pos).start()
    kv[0, c] = mm(enc_ref[...], wc[member]).astype(BF16)
    core_copy(0, c).start()
    q_load.wait()

    for j in range(1, Q):
        send_tokens(j).wait_send()
        for p in range(pairs):
            pair_copy(j, p, seq, (seq + j) % Q).wait_send()
    for p in range(pairs):
        def gone(zv, steps):
            for step in steps:
                for to in step[1]:
                    by_z(p, step[0], to).wait_send()

        at_z(gone)
        for zz in range(Z):
            by_x(p, zz, x).wait_send()
        for xx in range(2):
            by_c(p, xx, c).wait_send()

    def hand_on(first, last):
        for pos in range(first, last):
            kv_copy(pos).wait_recv()
            core_copy(pos, c).start()

    def other_core(first, last):
        for pos in range(first, last):
            core_copy(pos, 1 - c).wait_recv()

    half = NQ // 2
    BQ = max(own_rows, min(256, half))
    nb = BQ // own_rows
    tiles = half // BQ
    lane = lax.broadcasted_iota(jnp.int32, (own_rows, PAIR), 1)
    row = lax.broadcasted_iota(jnp.int32, (own_rows, PAIR), 0)
    diagonal = (lane % DH) == row
    source = span // 2 * Q + seq

    def part_copies(b, s):
        to = b * Q + s
        r = c * (S // 2) + b
        return (
            remote(o_tx.at[b], o_rx.at[source], o_send.at[to], o_recv.at[source], r, s),
            remote(l_tx.at[b], l_rx.at[source], l_send.at[to], l_recv.at[source], r, s),
        )

    def attend_over(rows, first, last):
        block = kv[first:last].reshape((last - first) * 2 * T, 2 * PAIR)
        return pair_attend(qc[rows], block[:, :PAIR], block[:, PAIR:])

    def early(i, carry):
        rows = pl.ds(pl.multiple_of(i * BQ, BQ), BQ)
        num, tot, peak = attend_over(rows, 0, SPLIT)
        early_num[rows] = num
        early_tot[rows] = tot
        early_peak[rows] = peak
        return carry

    def final(step, carry):
        i = step
        rows = pl.ds(pl.multiple_of(i * BQ, BQ), BQ)
        num, tot, peak = attend_over(rows, SPLIT, G)
        before = early_peak[rows]
        top = jnp.maximum(peak, before)
        old = jnp.exp(before - top)
        new = jnp.exp(peak - top)
        num = num * new + early_num[rows] * old
        tot = tot * new + early_tot[rows] * old
        part = (num / tot).astype(BF16)
        lse = top + jnp.log(tot)
        for k in range(nb):
            b = i * nb + k
            r = c * (S // 2) + b
            stat = jnp.sum(
                jnp.where(diagonal, lse[k * own_rows:(k + 1) * own_rows], 0.0), 0, keepdims=True
            )
            o_tx[b] = part[k * own_rows:(k + 1) * own_rows]
            l_tx[b] = stat

            @pl.when(r == span)
            def _():
                o_rx[source] = part[k * own_rows:(k + 1) * own_rows]
                l_rx[source] = stat

            for s in range(Q):
                @pl.when(r * Q + s != flat)
                def _():
                    for copy in part_copies(b, s):
                        copy.start()
        return carry

    hand_on(1, SPLIT)
    other_core(0, SPLIT)
    early(0, 0)
    hand_on(SPLIT, SPLIT + 1)
    lax.fori_loop(1, tiles, early, 0)
    hand_on(SPLIT + 1, G)
    other_core(SPLIT, G)
    lax.fori_loop(0, tiles, final, 0)

    senders = n // 2

    for pos in range(G):
        if pos:
            kv_copy(pos).wait_send()
        core_copy(pos, c).wait_send()

    def part_sent(to, carry):
        b = to // Q
        s = to % Q

        @pl.when((c * (S // 2) + b) * Q + s != flat)
        def _():
            for copy in part_copies(b, s):
                copy.wait_send()

        return carry

    lax.fori_loop(0, senders, part_sent, 0)

    def part_wait(src, carry):
        sender = src // Q * 2 + span // (S // 2)

        @pl.when(sender * Q + src % Q != flat)
        def _():
            remote(o_tx.at[0], o_rx.at[src], o_send.at[src], o_recv.at[src], c_peer, seq).wait_recv()
            remote(l_tx.at[0], l_rx.at[src], l_send.at[src], l_recv.at[src], c_peer, seq).wait_recv()

        return carry

    lax.fori_loop(0, senders, part_wait, 0)

    low = lane < DH

    def merge(g, carry):
        sources = [
            (a * (G // 2) + g // 2) * Q + s * 2 + g % 2 for a in range(S // G) for s in range(Q // 2)
        ]
        stats = [l_rx[src] for src in sources]
        top = functools.reduce(jnp.maximum, stats)
        weights = [jnp.exp(v - top) for v in stats]
        whole = functools.reduce(jnp.add, weights)
        total = jnp.zeros((own_rows, PAIR), F32)
        for src, weight in zip(sources, weights):
            spread = jnp.where(diagonal, weight / whole, 0.0)
            left = jnp.sum(jnp.where(low, spread, 0.0), 1, keepdims=True)
            right = jnp.sum(jnp.where(low, 0.0, spread), 1, keepdims=True)
            total += o_rx[src].astype(F32) * jnp.where(low, left, right)
        out_ref[:, pl.ds(pl.multiple_of(g * PAIR, PAIR), PAIR)] = total.astype(BF16)
        return carry

    lax.fori_loop(0, G, merge, 0, unroll=True)


def hand_over(enc_ref, part_ref, enc_out, part_out):
    enc_out[...] = enc_ref[...]
    part_out[...] = part_ref[...]


def solution(mesh):
    S = mesh.shape["span"]
    Q = mesh.shape["seq"]

    def per_device(tokens, w_qkv, w_out, w_cross, ln_gain, ln_bias, queries):
        T, D = tokens.shape
        NQ = queries.shape[0]
        R = w_qkv.shape[0]
        hcols = D // Q
        pairs = hcols // PAIR
        Z = S // 4
        G = D // PAIR
        own_rows = NQ // S
        any_spec = pl.BlockSpec(memory_space=pl.ANY)
        vmem_spec = pl.BlockSpec(memory_space=pltpu.VMEM)
        dma = pltpu.SemaphoreType.DMA
        n = S * Q
        results = pl.pallas_call(
            functools.partial(kernel, S, Q, NQ),
            out_shape=(
                jax.ShapeDtypeStruct((T, D), BF16),
                jax.ShapeDtypeStruct((own_rows, D), BF16),
            ),
            in_specs=[any_spec] * 4 + [vmem_spec] * 2 + [any_spec],
            out_specs=(vmem_spec, vmem_spec),
            scratch_shapes=[
                pltpu.VMEM((pairs, Z, 2, 2, R, 3 * PAIR), BF16),
                pltpu.VMEM((Q * T, D), BF16),
                pltpu.VMEM((pairs, Q * T, 3 * PAIR), BF16),
                pltpu.VMEM((D, D), BF16),
                pltpu.VMEM((G, D, 2 * PAIR), BF16),
                pltpu.VMEM((NQ // 2, PAIR), BF16),
                pltpu.VMEM((Q * T, hcols), BF16),
                pltpu.VMEM((Q, T, hcols), BF16),
                pltpu.VMEM((T, D), F32),
                pltpu.VMEM((G, T, 2 * PAIR), BF16),
                pltpu.VMEM((G, 2, T, 2 * PAIR), BF16),
                pltpu.VMEM((NQ // 2, PAIR), F32),
                pltpu.VMEM((NQ // 2, PAIR), F32),
                pltpu.VMEM((NQ // 2, PAIR), F32),
                pltpu.VMEM((S // 2, own_rows, PAIR), BF16),
                pltpu.VMEM((S // 2, 1, PAIR), F32),
                pltpu.VMEM((n // 2, own_rows, PAIR), BF16),
                pltpu.VMEM((n // 2, 1, PAIR), F32),
                dma((pairs, 3)), dma((3 + 2 * G,)),
                dma((pairs, Z, Z)), dma((pairs, Z)), dma((pairs, Z)), dma((pairs, Z)), dma((pairs, 2)), dma((pairs, 2)),
                dma((Q,)), dma((Q,)), dma((Q, pairs)), dma((Q, pairs)), dma((G,)), dma((G,)), dma((G,)), dma((G,)),
                dma((n // 2,)), dma((n // 2,)), dma((n // 2,)), dma((n // 2,)),
            ],
            compiler_params=pltpu.CompilerParams(
                collective_id=0, has_side_effects=True, vmem_limit_bytes=56 << 20
            ),
        )(tokens, w_qkv, w_out, w_cross, ln_gain.reshape(1, D), ln_bias.reshape(1, D), queries)
        return pl.pallas_call(
            hand_over,
            out_shape=tuple(jax.ShapeDtypeStruct(r.shape, r.dtype) for r in results),
            in_specs=[vmem_spec] * 2,
            out_specs=(vmem_spec, vmem_spec),
        )(*results)

    in_specs = (P(("span", "seq"), None), P("span", None), P(), P(), P(), P(), P())
    out_specs = (P(("span", "seq"), None), P("span", None))
    return jax.shard_map(
        per_device, mesh=mesh, in_specs=in_specs, out_specs=out_specs, check_vma=False
    )
```

```python
import functools

import jax
import jax.numpy as jnp
from jax import lax
from jax.experimental import pallas as pl
from jax.experimental.pallas import tpu as pltpu
from jax.sharding import PartitionSpec as P

DH = 64
PAIR = 2 * DH
score_scale = 0.125
F32 = jnp.float32
BF16 = jnp.bfloat16
MESH = pl.DeviceIdType.MESH
ORDER = (0, 4, 2, 1, 6, 5, 3, 7)
SPLIT = 4


def mm(a, b):
    return jnp.dot(a, b, preferred_element_type=F32)


def mm_t(a, b):
    return lax.dot_general(a, b, (((1,), (1,)), ((), ())), preferred_element_type=F32)


def pair_attend(query, key, value):
    lane = lax.broadcasted_iota(jnp.int32, (1, PAIR), 1)
    low = lane < DH
    low_f = jnp.where(low, 1.0, 0.0)
    low_b = low_f.astype(BF16)
    high_b = (1.0 - low_f).astype(BF16)
    scaled = query * jnp.asarray(score_scale, BF16)

    def one(own, other):
        scores = mm_t(scaled * own, key)
        peak = jnp.max(scores, -1, keepdims=True)
        probs = jnp.exp(scores - peak).astype(BF16)
        return mm(probs, value * own + other), peak

    first, first_peak = one(low_b, high_b)
    second, second_peak = one(high_b, low_b)
    numerator = jnp.where(low, first, second)
    total = pltpu.roll(jnp.where(low, second, first), DH, 1)
    return numerator, total, jnp.where(low, first_peak, second_peak)


def routes(Z):
    if Z == 4:
        return [
            [(0, [1]), (1, [], False), (2, [], True), (3, [], True)],
            [(1, [2, 0]), (0, [2, 3], False), (2, [0], False), (3, [], True)],
            [(2, [1, 3]), (3, [1, 0], False), (1, [3], False), (0, [], True)],
            [(3, [2]), (2, [], False), (1, [], True), (0, [], True)],
        ]
    return [
        [(z, [(z + k) % Z for k in range(1, Z)])] + [((z - k) % Z, [], False) for k in range(1, Z)]
        for z in range(Z)
    ]


def kernel(
    S, Q, NQ,
    tokens_ref, wqkv_ref, wout_ref, wcross_ref, gain_ref, bias_ref, queries_ref,
    enc_ref, out_ref,
    wbuf, tokall, qkv, wout, wc, qc, att, attn, res, kv_tx, kv,
    early_num, early_tot, early_peak, o_tx, l_tx, o_rx, l_rx,
    w_sem, local_sem, z_send, z_recv, x_send, x_recv, c_send, c_recv,
    tok_send, tok_recv, at_send, at_recv, kv_send, kv_recv, f_send, f_recv,
    o_send, o_recv, l_send, l_recv,
):
    T, D = tokens_ref.shape
    R = wqkv_ref.shape[0]
    hcols = D // Q
    pairs = hcols // PAIR
    Z = S // 4
    G = D // PAIR
    own_rows = NQ // S
    n = S * Q
    plan = routes(Z)
    span = lax.axis_index("span")
    seq = lax.axis_index("seq")
    z = span // 4
    x = (span // 2) % 2
    c = span % 2
    my_z = z % 2
    my_s = seq % 2
    member = my_z * 4 + x * 2 + my_s
    base = span - span % G
    flat = span * Q + seq

    w_loads = []
    for p in range(pairs):
        for j in range(3):
            copy = pltpu.make_async_copy(
                wqkv_ref.at[:, pl.ds(pl.multiple_of(j * D + seq * hcols + p * PAIR, PAIR), PAIR)],
                wbuf.at[p, z, x, c, :, pl.ds(j * PAIR, PAIR)],
                w_sem.at[p, j],
            )
            copy.start()
            w_loads.append(copy)

    loads = []

    def load(src, dst):
        copy = pltpu.make_async_copy(src, dst, local_sem.at[len(loads)])
        copy.start()
        loads.append(copy)
        return copy

    own_t = pl.ds(pl.multiple_of(seq * T, T), T)
    t_load = load(tokens_ref, tokall.at[own_t])

    barrier = pltpu.get_barrier_semaphore()

    def greet(to_span, to_seq):
        pl.semaphore_signal(
            barrier, inc=1, device_id={"span": to_span, "seq": to_seq}, device_id_type=MESH
        )

    x_peer = z * 4 + (1 - x) * 2 + c
    c_peer = z * 4 + x * 2 + (1 - c)

    for k in range(1, Z):
        greet((z + k) % Z * 4 + x * 2 + c, seq)
    greet(x_peer, seq)
    greet(c_peer, seq)
    for j in range(1, Q):
        greet(span, (seq + j) % Q)

    wo_load = load(wout_ref, wout)
    wc_loads = []
    for g in range(G):
        for half in range(2):
            wc_loads.append(
                load(
                    wcross_ref.at[:, pl.ds(half * D + g * PAIR, PAIR)],
                    wc.at[g, :, pl.ds(half * PAIR, PAIR)],
                )
            )
    q_load = load(
        queries_ref.at[
            pl.ds(pl.multiple_of(c * (NQ // 2), NQ // 2), NQ // 2),
            pl.ds(pl.multiple_of(member * PAIR, PAIR), PAIR),
        ],
        qc,
    )
    pl.semaphore_wait(barrier, Z + Q)

    def remote(src, dst, ssem, rsem, to_span, to_seq):
        return pltpu.make_async_remote_copy(
            src_ref=src, dst_ref=dst, send_sem=ssem, recv_sem=rsem,
            device_id={"span": to_span, "seq": to_seq}, device_id_type=MESH,
        )

    def by_z(p, zz, to):
        unit = wbuf.at[p, zz, x, c]
        return remote(
            unit, unit, z_send.at[p, zz, to], z_recv.at[p, zz], to * 4 + x * 2 + c, seq
        )

    def by_x(p, zz, xx):
        unit = wbuf.at[p, zz, xx, c]
        return remote(unit, unit, x_send.at[p, zz], x_recv.at[p, zz], x_peer, seq)

    def by_c(p, xx, cc):
        units = wbuf.at[p, :, xx, cc]
        return remote(units, units, c_send.at[p, xx], c_recv.at[p, xx], c_peer, seq)

    def send_tokens(j):
        mine = tokall.at[own_t]
        return remote(mine, mine, tok_send.at[j], tok_recv.at[seq], span, (seq + j) % Q)

    def at_z(action):
        for zv in range(Z):
            @pl.when(z == zv)
            def _():
                action(zv, plan[zv])

    def own(p):
        if p >= pairs:
            return
        for copy in w_loads[3 * p:3 * p + 3]:
            copy.wait()

        def go(zv, steps):
            for to in steps[0][1]:
                by_z(p, zv, to).start()

        at_z(go)
        by_x(p, z, x).start()
        if p == 0:
            t_load.wait()
            for j in range(1, Q):
                send_tokens(j).start()

    def arrive(p, second):
        if p >= pairs:
            return

        def go(zv, steps):
            for zz, onward, late in steps[1:]:
                if late == second:
                    by_z(p, zz, zv).wait_recv()
                    for to in onward:
                        by_z(p, zz, to).start()
                    by_x(p, zz, x).start()

        at_z(go)
        if second:
            by_c(p, x, c).start()

    def cross_over(p):
        if p >= pairs:
            return
        for zz in range(Z):
            by_x(p, zz, 1 - x).wait_recv()
        by_c(p, 1 - x, c).start()

    def project(p, owner):
        trows = pl.ds(pl.multiple_of(owner * T, T), T)
        w = wbuf[p].reshape(D, 3 * PAIR)
        qkv[p, trows] = mm(tokall[trows], w).astype(BF16)

    def project_own(p):
        if p >= pairs:
            return
        for xx in range(2):
            by_c(p, xx, 1 - c).wait_recv()
        if p < 2:
            project(p, seq)

    def attend(p, rows):
        num, tot, _ = pair_attend(
            qkv[p, rows, :PAIR], qkv[p, :, PAIR:2 * PAIR], qkv[p, :, 2 * PAIR:]
        )
        att[rows, p * PAIR:(p + 1) * PAIR] = (num / tot).astype(BF16)

    def pair_copy(j, p, at, owner):
        cols = pl.ds(p * PAIR, PAIR)
        return remote(
            att.at[pl.ds(pl.multiple_of(owner * T, T), T), cols], attn.at[at, :, cols],
            at_send.at[j, p], at_recv.at[at, p], span, owner,
        )

    def project_rest(p):
        if p >= pairs:
            return
        if p < 2:
            for j in range(1, Q):
                project(p, (seq + j) % Q)
        else:
            qkv[p] = mm(tokall[...], wbuf[p].reshape(D, 3 * PAIR)).astype(BF16)

    def attend_all(p):
        if p >= pairs:
            return
        if p < pairs - 1:
            for i in range(Q // 2):
                attend(p, pl.ds(2 * i * T, 2 * T))
            for j in range(1, Q):
                pair_copy(j, p, seq, (seq + j) % Q).start()
        else:
            for j in range(1, Q):
                owner = (seq + j) % Q
                attend(p, pl.ds(pl.multiple_of(owner * T, T), T))
                pair_copy(j, p, seq, owner).start()
            attend(p, own_t)

    def tokens_arrive():
        for j in range(1, Q):
            other = (seq + j) % Q
            theirs = tokall.at[pl.ds(pl.multiple_of(other * T, T), T)]
            remote(theirs, theirs, tok_send.at[j], tok_recv.at[other], span, other).wait_recv()

    own(0)
    own(1)
    arrive(0, False)
    own(2)
    arrive(0, True)
    arrive(1, False)
    own(3)
    arrive(1, True)
    arrive(2, False)
    cross_over(0)
    arrive(2, True)
    arrive(3, False)
    cross_over(1)
    arrive(3, True)
    project_own(0)
    cross_over(2)
    project_own(1)
    tokens_arrive()
    project_rest(0)
    attend_all(0)
    project_own(2)
    project_rest(1)
    attend_all(1)
    cross_over(3)
    project_rest(2)
    attend_all(2)
    project_own(3)
    project_rest(3)
    attend_all(3)
    wo_load.wait()
    NT = 256

    done = hcols - PAIR

    def wout_rows(j_seq, first, count):
        return pl.ds(pl.multiple_of(j_seq * hcols + first, PAIR), count)

    def own_part(i, carry):
        cols = pl.ds(pl.multiple_of(i * NT, NT), NT)
        part = mm(att[own_t], wout[wout_rows(seq, 0, hcols), cols])
        res[:, cols] = tokall[own_t, cols].astype(F32) + part
        return carry

    def their_part(owner, i, carry):
        cols = pl.ds(pl.multiple_of(i * NT, NT), NT)
        res[:, cols] += mm(attn[owner, :, :done], wout[wout_rows(owner, 0, done), cols])
        return carry

    lax.fori_loop(0, D // NT, own_part, 0, unroll=True)
    others = [(seq + j) % Q for j in range(1, Q)]
    for j, owner in enumerate(others, 1):
        for p in range(pairs - 1):
            pair_copy(j, p, owner, owner).wait_recv()
        if done:
            lax.fori_loop(0, D // NT, functools.partial(their_part, owner), 0, unroll=True)
    for j, owner in enumerate(others, 1):
        pair_copy(j, pairs - 1, owner, owner).wait_recv()
    LT = T // 2

    def norm(i, carry):
        rows = pl.ds(pl.multiple_of(i * LT, LT), LT)
        r = res[rows]
        for owner in others:
            r += mm(attn[owner, rows, done:], wout[wout_rows(owner, done, PAIR)])
        center = r - jnp.mean(r, -1, keepdims=True)
        spread = jnp.mean(center * center, -1, keepdims=True)
        enc_ref[rows] = (
            center * lax.rsqrt(spread + 1e-05) * gain_ref[...] + bias_ref[...]
        ).astype(BF16)
        return carry

    lax.fori_loop(0, T // LT, norm, 0, unroll=True)

    for copy in wc_loads:
        copy.wait()

    def chip_at(pos):
        flip = ORDER[pos]
        s1 = 1 - my_s if flip & 1 else my_s
        x1 = 1 - x if flip & 2 else x
        z1 = 1 - my_z if flip & 4 else my_z
        return z1 * 4 + x1 * 2 + s1, base + z1 * 4 + x1 * 2 + c, seq - my_s + s1

    def kv_copy(pos):
        _, to_span, to_seq = chip_at(pos)
        return remote(
            kv_tx.at[pos], kv.at[pos, c], kv_send.at[pos], kv_recv.at[pos], to_span, to_seq
        )

    def core_copy(pos, cc):
        block = kv.at[pos, cc]
        return remote(block, block, f_send.at[pos], f_recv.at[pos], c_peer, seq)

    for pos in range(1, G):
        kv_tx[pos] = mm(enc_ref[...], wc[chip_at(pos)[0]]).astype(BF16)
        kv_copy(pos).start()
    kv[0, c] = mm(enc_ref[...], wc[member]).astype(BF16)
    core_copy(0, c).start()
    q_load.wait()

    for j in range(1, Q):
        send_tokens(j).wait_send()
        for p in range(pairs):
            pair_copy(j, p, seq, (seq + j) % Q).wait_send()
    for p in range(pairs):
        def gone(zv, steps):
            for step in steps:
                for to in step[1]:
                    by_z(p, step[0], to).wait_send()

        at_z(gone)
        for zz in range(Z):
            by_x(p, zz, x).wait_send()
        for xx in range(2):
            by_c(p, xx, c).wait_send()

    def hand_on(first, last):
        for pos in range(first, last):
            kv_copy(pos).wait_recv()
            core_copy(pos, c).start()

    def other_core(first, last):
        for pos in range(first, last):
            core_copy(pos, 1 - c).wait_recv()

    half = NQ // 2
    BQ = max(own_rows, min(256, half))
    nb = BQ // own_rows
    tiles = half // BQ
    lane = lax.broadcasted_iota(jnp.int32, (own_rows, PAIR), 1)
    row = lax.broadcasted_iota(jnp.int32, (own_rows, PAIR), 0)
    diagonal = (lane % DH) == row
    source = span // 2 * Q + seq

    def part_copies(b, s):
        to = b * Q + s
        r = c * (S // 2) + b
        return (
            remote(o_tx.at[b], o_rx.at[source], o_send.at[to], o_recv.at[source], r, s),
            remote(l_tx.at[b], l_rx.at[source], l_send.at[to], l_recv.at[source], r, s),
        )

    def attend_over(rows, first, last):
        block = kv[first:last].reshape((last - first) * 2 * T, 2 * PAIR)
        return pair_attend(qc[rows], block[:, :PAIR], block[:, PAIR:])

    def early(i, carry):
        rows = pl.ds(pl.multiple_of(i * BQ, BQ), BQ)
        num, tot, peak = attend_over(rows, 0, SPLIT)
        early_num[rows] = num
        early_tot[rows] = tot
        early_peak[rows] = peak
        return carry

    def final(step, carry):
        i = step
        rows = pl.ds(pl.multiple_of(i * BQ, BQ), BQ)
        num, tot, peak = attend_over(rows, SPLIT, G)
        before = early_peak[rows]
        top = jnp.maximum(peak, before)
        old = jnp.exp(before - top)
        new = jnp.exp(peak - top)
        num = num * new + early_num[rows] * old
        tot = tot * new + early_tot[rows] * old
        part = (num / tot).astype(BF16)
        lse = top + jnp.log(tot)
        for k in range(nb):
            b = i * nb + k
            r = c * (S // 2) + b
            stat = jnp.sum(
                jnp.where(diagonal, lse[k * own_rows:(k + 1) * own_rows], 0.0), 0, keepdims=True
            )
            o_tx[b] = part[k * own_rows:(k + 1) * own_rows]
            l_tx[b] = stat

            @pl.when(r == span)
            def _():
                o_rx[source] = part[k * own_rows:(k + 1) * own_rows]
                l_rx[source] = stat

            for s in range(Q):
                @pl.when(r * Q + s != flat)
                def _():
                    for copy in part_copies(b, s):
                        copy.start()
        return carry

    hand_on(1, SPLIT)
    other_core(0, SPLIT)
    early(0, 0)
    hand_on(SPLIT, SPLIT + 1)
    lax.fori_loop(1, tiles, early, 0)
    hand_on(SPLIT + 1, G)
    other_core(SPLIT, G)
    lax.fori_loop(0, tiles, final, 0)

    senders = n // 2

    for pos in range(G):
        if pos:
            kv_copy(pos).wait_send()
        core_copy(pos, c).wait_send()

    def part_sent(to, carry):
        b = to // Q
        s = to % Q

        @pl.when((c * (S // 2) + b) * Q + s != flat)
        def _():
            for copy in part_copies(b, s):
                copy.wait_send()

        return carry

    lax.fori_loop(0, senders, part_sent, 0)

    def part_wait(src, carry):
        sender = src // Q * 2 + span // (S // 2)

        @pl.when(sender * Q + src % Q != flat)
        def _():
            remote(o_tx.at[0], o_rx.at[src], o_send.at[src], o_recv.at[src], c_peer, seq).wait_recv()
            remote(l_tx.at[0], l_rx.at[src], l_send.at[src], l_recv.at[src], c_peer, seq).wait_recv()

        return carry

    lax.fori_loop(0, senders, part_wait, 0)

    low = lane < DH

    def merge(g, carry):
        sources = [
            (a * (G // 2) + g // 2) * Q + s * 2 + g % 2 for a in range(S // G) for s in range(Q // 2)
        ]
        stats = [l_rx[src] for src in sources]
        top = functools.reduce(jnp.maximum, stats)
        weights = [jnp.exp(v - top) for v in stats]
        whole = functools.reduce(jnp.add, weights)
        total = jnp.zeros((own_rows, PAIR), F32)
        for src, weight in zip(sources, weights):
            spread = jnp.where(diagonal, weight / whole, 0.0)
            left = jnp.sum(jnp.where(low, spread, 0.0), 1, keepdims=True)
            right = jnp.sum(jnp.where(low, 0.0, spread), 1, keepdims=True)
            total += o_rx[src].astype(F32) * jnp.where(low, left, right)
        out_ref[:, pl.ds(pl.multiple_of(g * PAIR, PAIR), PAIR)] = total.astype(BF16)
        return carry

    lax.fori_loop(0, G, merge, 0, unroll=True)


def hand_over(enc_ref, part_ref, enc_out, part_out):
    enc_out[...] = enc_ref[...]
    part_out[...] = part_ref[...]


def solution(mesh):
    S = mesh.shape["span"]
    Q = mesh.shape["seq"]

    def per_device(tokens, w_qkv, w_out, w_cross, ln_gain, ln_bias, queries):
        T, D = tokens.shape
        NQ = queries.shape[0]
        R = w_qkv.shape[0]
        hcols = D // Q
        pairs = hcols // PAIR
        Z = S // 4
        G = D // PAIR
        own_rows = NQ // S
        any_spec = pl.BlockSpec(memory_space=pl.ANY)
        vmem_spec = pl.BlockSpec(memory_space=pltpu.VMEM)
        dma = pltpu.SemaphoreType.DMA
        n = S * Q
        results = pl.pallas_call(
            functools.partial(kernel, S, Q, NQ),
            out_shape=(
                jax.ShapeDtypeStruct((T, D), BF16),
                jax.ShapeDtypeStruct((own_rows, D), BF16),
            ),
            in_specs=[any_spec] * 4 + [vmem_spec] * 2 + [any_spec],
            out_specs=(vmem_spec, vmem_spec),
            scratch_shapes=[
                pltpu.VMEM((pairs, Z, 2, 2, R, 3 * PAIR), BF16),
                pltpu.VMEM((Q * T, D), BF16),
                pltpu.VMEM((pairs, Q * T, 3 * PAIR), BF16),
                pltpu.VMEM((D, D), BF16),
                pltpu.VMEM((G, D, 2 * PAIR), BF16),
                pltpu.VMEM((NQ // 2, PAIR), BF16),
                pltpu.VMEM((Q * T, hcols), BF16),
                pltpu.VMEM((Q, T, hcols), BF16),
                pltpu.VMEM((T, D), F32),
                pltpu.VMEM((G, T, 2 * PAIR), BF16),
                pltpu.VMEM((G, 2, T, 2 * PAIR), BF16),
                pltpu.VMEM((NQ // 2, PAIR), F32),
                pltpu.VMEM((NQ // 2, PAIR), F32),
                pltpu.VMEM((NQ // 2, PAIR), F32),
                pltpu.VMEM((S // 2, own_rows, PAIR), BF16),
                pltpu.VMEM((S // 2, 1, PAIR), F32),
                pltpu.VMEM((n // 2, own_rows, PAIR), BF16),
                pltpu.VMEM((n // 2, 1, PAIR), F32),
                dma((pairs, 3)), dma((3 + 2 * G,)),
                dma((pairs, Z, Z)), dma((pairs, Z)), dma((pairs, Z)), dma((pairs, Z)), dma((pairs, 2)), dma((pairs, 2)),
                dma((Q,)), dma((Q,)), dma((Q, pairs)), dma((Q, pairs)), dma((G,)), dma((G,)), dma((G,)), dma((G,)),
                dma((n // 2,)), dma((n // 2,)), dma((n // 2,)), dma((n // 2,)),
            ],
            compiler_params=pltpu.CompilerParams(
                collective_id=0, has_side_effects=True, vmem_limit_bytes=56 << 20
            ),
        )(tokens, w_qkv, w_out, w_cross, ln_gain.reshape(1, D), ln_bias.reshape(1, D), queries)
        return pl.pallas_call(
            hand_over,
            out_shape=tuple(jax.ShapeDtypeStruct(r.shape, r.dtype) for r in results),
            in_specs=[vmem_spec] * 2,
            out_specs=(vmem_spec, vmem_spec),
        )(*results)

    in_specs = (P(("span", "seq"), None), P("span", None), P(), P(), P(), P(), P())
    out_specs = (P(("span", "seq"), None), P("span", None))
    return jax.shard_map(
        per_device, mesh=mesh, in_specs=in_specs, out_specs=out_specs, check_vma=False
    )
```
